32 devices in a mesh: gx: 4 (over z), gy: 4 (over y, x), gz: 2 (over core).
Axes of the slice: x: 2, y: 2, z: 4, core: 2. Of those that a mesh axis runs over, the one named last changes fastest.
Arguments:
- places: float32 [256, 3], P(('gx', 'gy', 'gz')), may hold values from 0 to 1
- scalars: float32 [256, 256], P(('gx', 'gy', 'gz')), may hold values from -6 to 6
- vectors: float32 [256, 3, 256], P(('gx', 'gy', 'gz')), may hold values from -6 to 6
- species: int32 [256], P(('gx', 'gy', 'gz')), may hold values from 0 to 3
- bound_rows: int32 [256], P(('gx', 'gy', 'gz')), may hold values from 0 to 7, as said below
- bound_count: int32 [32], P(('gx', 'gy', 'gz')), may hold values from 4 to 8, as said below
- neighbour_ids: int32 [16, 256], P(None, ('gx', 'gy', 'gz')), may hold values from 0 to 223, as said below
- neighbour_count: int32 [256], P(('gx', 'gy', 'gz')), may hold values from 3 to 16, as said below
- radial_first: bfloat16 [8, 64], replicated, may hold values from -2 to 2
- radial_second: bfloat16 [64, 64], replicated, may hold values from -0.75 to 0.75
- radial_third: bfloat16 [64, 1536], replicated, may hold values from -0.75 to 0.75
- energy_table: float32 [4, 256], replicated, may hold values from -6 to 6
- vector_gains: float32 [256], replicated, may hold values from -3 to 3
Outputs:
- atom_energy: float32 [256], P(('gx', 'gy', 'gz'))
- forces: float32 [256, 3], P(('gx', 'gy', 'gz'))
- grad_scalars: float32 [256, 256], P(('gx', 'gy', 'gz'))
- grad_vectors: float32 [256, 3, 256], P(('gx', 'gy', 'gz'))
The draws below stay inside these ranges and needn't reach their ends.
Inputs may be any that keep to these rules, and one draw needn't show every extreme that they name: `bound_rows`: per domain, 8 distinct indices of its own atoms (0 to 7). `bound_count`: some domain has all 8 slots live. `neighbour_ids`: below 8: an owned atom other than the atom itself; otherwise 8 + t * 8 + b for ghost block t, never the centre block 13, and any slot b, live or not. `neighbour_count`: slots k below the count are listed neighbours. Domains differ in their largest count; some atom has 16.
All inputs are finite; a program needn't handle non-finite values.
Results may differ from the reference program's by a relative error of at most 0.014.
Values sent between devices are 32-bit elements; how exact they have to be, the bound alone decides.
No kernel may reach another device: no remote copies, remote signals or barrier semaphores. Data moves between devices by JAX's collectives and lax.ppermute only.
A program may use at most 64 MiB of HBM per device.

```python
import jax
import jax.numpy as jnp
from jax import lax

ATOMS_DEV = 8
BOUNDARY = 8
NEIGHBOURS = 16
CHANNELS = 256
RADIAL_HIDDEN = 64
GAUSSIANS = 8
SPECIES = 4
RADIAL_OUT = 1536
ATOMS_ALL = 256
N_GX = 4
N_GY = 4
N_GZ = 2


def draw_bound_rows(key, part):
    domains = N_GX * N_GY * N_GZ
    scores = jax.random.randint(key, (domains, ATOMS_DEV), 0, 1 << 20) * ATOMS_DEV + jnp.arange(ATOMS_DEV).astype(jnp.int32)[None]
    order = jnp.argsort(scores, axis=1, stable=True)
    return order[:, :BOUNDARY].reshape(-1).astype(jnp.int32)


def draw_bound_count(key, part):
    domains = N_GX * N_GY * N_GZ
    key_one, key_two = jax.random.split(jax.random.fold_in(key, 11))
    counts = jax.random.randint(key_one, (domains,), BOUNDARY // 2, BOUNDARY + 1)
    fullest = jax.random.randint(key_two, (), 0, domains)
    return jnp.where(jnp.arange(domains) == fullest, BOUNDARY, counts).astype(jnp.int32)


def draw_neighbour_ids(key, part):
    domains = N_GX * N_GY * N_GZ
    total = domains * ATOMS_DEV
    keys = jax.random.split(jax.random.fold_in(key, 23), 4)
    local = jnp.arange(total).astype(jnp.int32) % ATOMS_DEV
    pick = jax.random.randint(keys[0], (NEIGHBOURS, total), 0, 10)
    owned_pick = (local[None] + 1 + jax.random.randint(keys[1], (NEIGHBOURS, total), 0, ATOMS_DEV - 1)) % ATOMS_DEV
    block = jax.random.randint(keys[2], (NEIGHBOURS, total), 0, 26)
    block = block + (block >= 13).astype(jnp.int32)
    slot = jax.random.randint(keys[3], (NEIGHBOURS, total), 0, BOUNDARY)
    ghost_pick = ATOMS_DEV + block * BOUNDARY + slot
    return jnp.where(pick < 3, owned_pick, ghost_pick).astype(jnp.int32)


def draw_neighbour_count(key, part):
    domains = N_GX * N_GY * N_GZ
    keys = jax.random.split(jax.random.fold_in(key, 37), 4)
    ceiling = jax.random.randint(keys[0], (domains,), NEIGHBOURS // 4, NEIGHBOURS + 1)
    fullest = jax.random.randint(keys[1], (), 0, domains)
    ceiling = jnp.where(jnp.arange(domains) == fullest, NEIGHBOURS, ceiling)
    halfway = ceiling // 2
    spread = jax.random.randint(keys[2], (domains, ATOMS_DEV), 0, 1 << 20)
    counts = halfway[:, None] + 1 + spread % (ceiling - halfway)[:, None]
    peak = jax.random.randint(keys[3], (domains,), 0, ATOMS_DEV)
    counts = jnp.where(jnp.arange(ATOMS_DEV)[None] == peak[:, None], ceiling[:, None], counts)
    return counts.reshape(-1).astype(jnp.int32)


def plant(values, rng, low, top_value):
    place = [jax.random.randint(jax.random.fold_in(rng, axis), (), 0, length) for axis, length in enumerate(values.shape)]
    longest = values.shape.index(max(values.shape))
    next_to = place[:longest] + [(place[longest] + 1) % values.shape[longest]] + place[longest + 1:]
    return values.at[tuple(place)].set(low).at[tuple(next_to)].set(top_value)


def level_of(stream_key, extent, shards, smallest, high):
    gain = 1.0
    for axis_at, parts in shards:
        draws = jax.random.uniform(jax.random.fold_in(jax.random.fold_in(stream_key, 6), axis_at), (parts,), jnp.float32, smallest / len(shards), high / len(shards))
        gain = gain * jnp.repeat(jnp.exp(draws), extent[axis_at] // parts).reshape((-1,) + (1,) * (len(extent) - 1 - axis_at))
    return gain


def normal_values(rng, dims, scale, limit, cuts=(), kind=jnp.bfloat16):
    entries = jax.random.normal(rng, dims, jnp.float32) * scale
    if len(cuts) > 0:
        entries = level_of(rng, dims, cuts, -0.22, 0.18) * entries
    return jnp.clip(entries, min=-limit, max=limit).astype(kind)


def setup_inputs(seed: int = 0) -> dict:
    key_list = jax.random.split(jax.random.key(seed), 14)
    return {
        "places": jnp.clip(1.0 * jax.random.uniform(key_list[0], (ATOMS_ALL, 3), jnp.float32) ** level_of(key_list[0], (ATOMS_ALL, 3), ((0, 32),), -0.2, 0.2), 0.0, 1.0),
        "scalars": normal_values(key_list[1], (ATOMS_ALL, CHANNELS), 1.0, 6.0, ((0, 32),), jnp.float32),
        "vectors": normal_values(key_list[2], (ATOMS_ALL, 3, CHANNELS), 1.0, 6.0, ((0, 32),), jnp.float32),
        "species": plant(jax.random.randint(key_list[3], (ATOMS_ALL,), 0, SPECIES), jax.random.fold_in(key_list[3], 1), 0, SPECIES - 1).astype(jnp.int32),
        "bound_rows": draw_bound_rows(jax.random.fold_in(key_list[13], 71), 0),
        "bound_count": draw_bound_count(jax.random.fold_in(key_list[13], 71), 0),
        "neighbour_ids": draw_neighbour_ids(jax.random.fold_in(key_list[13], 71), 0),
        "neighbour_count": draw_neighbour_count(jax.random.fold_in(key_list[13], 71), 0),
        "radial_first": normal_values(key_list[8], (GAUSSIANS, RADIAL_HIDDEN), GAUSSIANS ** -0.5, 2.0),
        "radial_second": normal_values(key_list[9], (RADIAL_HIDDEN, RADIAL_HIDDEN), RADIAL_HIDDEN ** -0.5, 0.75),
        "radial_third": normal_values(key_list[10], (RADIAL_HIDDEN, RADIAL_OUT), RADIAL_HIDDEN ** -0.5, 0.75),
        "energy_table": normal_values(key_list[11], (SPECIES, CHANNELS), 1.0, 6.0, (), jnp.float32),
        "vector_gains": normal_values(key_list[12], (CHANNELS,), 0.5, 3.0, (), jnp.float32),
    }


SOFTENING = 0.25
SHARPNESS = 2.0
FIRST_CENTRE = 0.5
SPACING = 0.4
EDGE = 1.0

def edge_messages(row_table, index_rows, usable, radial_first, radial_second, radial_third):
    slot_rows, atoms_here = index_rows.shape
    channels = (row_table.shape[1] - 3) // 4
    owned_places = row_table[:atoms_here, :3]
    far_rows = row_table[index_rows]
    separation = far_rows[:, :, :3] - owned_places[None]
    distance = jnp.sqrt(lax.optimization_barrier(jnp.sum(separation * separation, axis=2)) + SOFTENING)
    direction = separation / distance[:, :, None]
    centres = FIRST_CENTRE + SPACING * jnp.arange(radial_first.shape[0]).astype(jnp.float32)
    gauss_basis = jnp.exp(-SHARPNESS * (distance[:, :, None] - centres) ** 2)
    flat_basis = gauss_basis.reshape(slot_rows * atoms_here, -1).astype(jnp.bfloat16)
    hidden_one = jax.nn.silu(jnp.dot(flat_basis, radial_first, preferred_element_type=jnp.float32)).astype(jnp.bfloat16)
    hidden_two = jax.nn.silu(jnp.dot(hidden_one, radial_second, preferred_element_type=jnp.float32)).astype(jnp.bfloat16)
    path_weights = jnp.dot(hidden_two, radial_third, preferred_element_type=jnp.float32).reshape(slot_rows, atoms_here, 6, channels)
    far_scalars = far_rows[:, :, 3:3 + channels]
    far_vectors = far_rows[:, :, 3 + channels:].reshape(slot_rows, atoms_here, 3, channels)
    projected = lax.optimization_barrier(jnp.sum(direction[:, :, :, None] * far_vectors, axis=2))
    crossed = jnp.stack([far_vectors[:, :, 1] * direction[:, :, 2:3] - far_vectors[:, :, 2] * direction[:, :, 1:2], far_vectors[:, :, 2] * direction[:, :, 0:1] - far_vectors[:, :, 0] * direction[:, :, 2:3], far_vectors[:, :, 0] * direction[:, :, 1:2] - far_vectors[:, :, 1] * direction[:, :, 0:1]], axis=2)
    scalar_message = path_weights[:, :, 0] * far_scalars + path_weights[:, :, 1] * projected
    vector_message = path_weights[:, :, 2:3] * far_scalars[:, :, None] * direction[:, :, :, None] + path_weights[:, :, 3:4] * far_vectors + path_weights[:, :, 4:5] * crossed + path_weights[:, :, 5:6] * (direction[:, :, :, None] * projected[:, :, None] - far_vectors / 3.0)
    weight = usable[:, :, None]
    return (lax.optimization_barrier(jnp.sum(weight * scalar_message, axis=0)), lax.optimization_barrier(jnp.sum(weight[:, :, :, None] * vector_message, axis=0)))

def atom_energy_of(scalar_out, vector_out, species_here, energy_table, vector_gains):
    channels = scalar_out.shape[1]
    onehot = (species_here[:, None] == jnp.arange(energy_table.shape[0]).astype(jnp.int32)[None]).astype(jnp.float32)
    species_coeff = jnp.dot(onehot, energy_table, precision=lax.Precision.HIGHEST)
    squares = lax.optimization_barrier(jnp.sum(vector_out * vector_out, axis=1))
    return (lax.optimization_barrier(jnp.sum(species_coeff * jax.nn.silu(scalar_out), axis=1)) + lax.optimization_barrier(jnp.sum(vector_gains * squares, axis=1))) * channels ** (-0.25)

def reference(places, scalars, vectors, species, bound_rows, bound_count, neighbour_ids, neighbour_count, radial_first, radial_second, radial_third, energy_table, vector_gains):
    domains = N_GX * N_GY * N_GZ
    scale = NEIGHBOURS ** (-0.5)
    ids_all = neighbour_ids.reshape(NEIGHBOURS, domains, ATOMS_DEV).transpose(1, 0, 2)
    usable_all = (jnp.arange(NEIGHBOURS).astype(jnp.int32)[None, :, None] < neighbour_count.reshape(domains, 1, ATOMS_DEV)).astype(jnp.float32)
    species_all = species.reshape(domains, ATOMS_DEV)
    boundary_idx = bound_rows.reshape(domains, BOUNDARY)
    alive_mask = (jnp.arange(BOUNDARY).astype(jnp.int32)[None] < bound_count[:, None]).astype(jnp.float32)

    def one_domain(inputs):
        row_table, ids_here, usable_here, species_here = inputs
        summed_scalar, summed_vector = edge_messages(row_table, ids_here, usable_here, radial_first, radial_second, radial_third)
        owned_rows = row_table[:ATOMS_DEV]
        scalar_out = owned_rows[:, 3:3 + CHANNELS] + scale * summed_scalar
        vector_out = owned_rows[:, 3 + CHANNELS:].reshape(ATOMS_DEV, 3, CHANNELS) + scale * summed_vector
        return atom_energy_of(scalar_out, vector_out, species_here, energy_table, vector_gains)

    def all_energy(places_in, scalars_in, vectors_in):
        owned_rows = jnp.concatenate([places_in, scalars_in, vectors_in.reshape(ATOMS_ALL, 3 * CHANNELS)], axis=1)
        owned_rows = owned_rows.reshape(domains, ATOMS_DEV, -1)
        packets = jnp.take_along_axis(owned_rows, boundary_idx[:, :, None], axis=1) * alive_mask[:, :, None]
        packet_grid = packets.reshape(N_GX, N_GY, N_GZ, BOUNDARY, -1)
        blocks = []
        for along_x in (-1, 0, 1):
            for along_y in (-1, 0, 1):
                for along_z in (-1, 0, 1):
                    rolled = jnp.roll(packet_grid, (-along_x, -along_y, -along_z), (0, 1, 2))
                    displace = jnp.array([along_x, along_y, along_z], jnp.float32) * EDGE
                    rolled = jnp.concatenate([rolled[..., :3] + displace, rolled[..., 3:]], axis=-1)
                    blocks.append(rolled.reshape(domains, BOUNDARY, -1))
        ghosts = jnp.concatenate(blocks, axis=1)
        tables = jnp.concatenate([owned_rows, ghosts], axis=1)
        energies = lax.map(jax.checkpoint(one_domain), (tables, ids_all, usable_all, species_all))
        return energies.reshape(-1)
    energies, pullback = jax.vjp(all_energy, places, scalars, vectors)
    grad_places, grad_scalars, grad_vectors = pullback(jnp.ones_like(energies))
    return (energies, -grad_places, grad_scalars, grad_vectors)
```

```python
import functools

import jax
import jax.numpy as jnp
from jax import lax
from jax.experimental import pallas as pl
from jax.experimental.pallas import tpu as pltpu
from jax.sharding import PartitionSpec as P

SOFTENING = 0.25
SHARPNESS = 2.0
FIRST_CENTRE = 0.5
SPACING = 0.4
EDGE = 1.0
LANES = 128
HIGHEST = lax.Precision.HIGHEST
AXES = ("gx", "gy", "gz")


def dot(a, b, dims, precision=None):
    return lax.dot_general(
        a, b, ((dims[:1], dims[1:]), ((), ())), precision=precision,
        preferred_element_type=jnp.float32,
    )


def sides(size):
    if size == 1:
        return []
    if size == 2:
        return [[(0, 1), (1, 0)]]
    if size % 2:
        return [[((i + 1) % size, i) for i in range(size)], [(i, (i + 1) % size) for i in range(size)]]
    pairs = [[(i, (i + 1) % size) for i in range(first, size, 2)] for first in (0, 1)]
    return [half + [(b, a) for a, b in half] for half in pairs]


def slot_of(offset, axis):
    size = lax.axis_size(axis)
    if size == 1:
        return jnp.zeros_like(offset)
    if size == 2:
        return jnp.abs(offset)
    parity = lax.axis_index(axis) % 2 if size % 2 == 0 else 0
    ahead = 1 - 2 * parity
    return jnp.where(offset == 0, 0, jnp.where(offset == ahead, 1, 2))


def swap(value, axis, pairs):
    return lax.ppermute(value, axis, pairs)


def inverse(pairs):
    return [(b, a) for a, b in pairs]


def pack_kernel(bound_rows, bound_count, places, scalars, vectors, out):
    boundary = bound_rows.shape[0]
    channels = scalars.shape[1]
    halves = channels // LANES
    out[4 * halves * boundary :, :] = jnp.zeros((boundary, LANES), jnp.float32)
    for slot in range(boundary):
        atom = bound_rows[slot]
        alive = jnp.where(slot < bound_count[0], 1.0, 0.0).astype(jnp.float32)
        rows = [scalars[pl.ds(atom, 1), :]] + [vectors[atom, a : a + 1, :] for a in range(3)]
        for part, row in enumerate(rows):
            row = row * alive
            for h in range(halves):
                at = (part * halves + h) * boundary + slot
                out[at : at + 1, :] = row[:, h * LANES : (h + 1) * LANES]
        at = 4 * halves * boundary + slot
        out[at : at + 1, 0:3] = places[pl.ds(atom, 1), :] * alive


def sigmoid(x):
    return 1.0 / (1.0 + jnp.exp(-x))


def core_kernel(
    geometry,
    species, row_of, displace, usable, places, scalars, vectors, first, second, third,
    energy_table, gains, *rest,
):
    atoms, slots, channels, blocks, tables = geometry
    ghosts = rest[:tables]
    energies, own_out = rest[tables : tables + 2]
    grads = rest[tables + 2 : 2 * tables + 2]
    table, weights, far, steer, coeff, place_rows, dfar, dweights, dsteer = rest[2 * tables + 2 :]
    halves = channels // LANES
    chunks = 4 * halves
    edges = atoms * slots
    packet = (chunks + 1) * atoms
    scale = slots ** (-0.5)
    readout = channels ** (-0.25)
    rows = sum(blocks) * atoms
    f32, bf16 = jnp.float32, jnp.bfloat16

    def pieces(chunk, own):
        parts = []
        for which, ref in enumerate(ghosts):
            for block in range(blocks[which]):
                if which == 0 and block == 0:
                    parts.append(own)
                else:
                    at = block * packet + chunk * atoms
                    parts.append(ref[at : at + atoms, :])
        return jnp.concatenate(parts, axis=0)

    row_index = lax.broadcasted_iota(jnp.int32, (rows, edges), 0)
    centre = lax.broadcasted_iota(jnp.int32, (rows, edges), 1) % atoms
    chosen = (row_index == row_of[...]).astype(f32)
    picks = chosen.astype(bf16)
    contrast = chosen - (row_index == centre).astype(f32)

    place_rows[...] = jnp.zeros((atoms, LANES), f32)
    place_rows[:, 0:3] = places[...]
    spots = pieces(chunks, place_rows[...])
    apart = dot(spots, contrast, (0, 0), HIGHEST)[0:8, :] + displace[...]
    distance = jnp.sqrt(jnp.sum(apart * apart, axis=0, keepdims=True) + SOFTENING)
    direction = apart / distance
    centres = FIRST_CENTRE + SPACING * lax.broadcasted_iota(jnp.int32, (first.shape[0], edges), 0).astype(f32)
    off = distance - centres
    gauss = jnp.exp(-SHARPNESS * off * off)
    pre_one = dot(first[...], gauss.astype(bf16), (0, 0))
    sig_one = sigmoid(pre_one)
    hidden_one = (pre_one * sig_one).astype(bf16)
    pre_two = dot(second[...], hidden_one, (0, 0))
    sig_two = sigmoid(pre_two)
    hidden_two = (pre_two * sig_two * usable[...]).astype(bf16)
    weights[...] = dot(hidden_two, third[...], (0, 0))
    spread = (
        lax.broadcasted_iota(jnp.int32, (8, 3 * LANES), 1) // LANES
        == lax.broadcasted_iota(jnp.int32, (8, 3 * LANES), 0)
    ).astype(f32)
    steer[...] = dot(direction, spread, (0, 0), HIGHEST)

    for part in range(4):
        for h in range(halves):
            chunk = part * halves + h
            lanes = slice(h * LANES, (h + 1) * LANES)
            own = scalars[:, lanes] if part == 0 else vectors[:, part - 1, lanes]
            table[:, chunk * LANES : (chunk + 1) * LANES] = pieces(chunk, own).astype(bf16)
    far[...] = dot(picks, table[...], (0, 0))

    tile = 2 * atoms
    steps = edges // tile

    def edge_inputs(step, h):
        at = slice(step * tile, (step + 1) * tile)
        s = far[at, h * LANES : (h + 1) * LANES]
        v = [far[at, ((1 + a) * halves + h) * LANES : ((1 + a) * halves + h + 1) * LANES] for a in range(3)]
        u = [steer[at, a * LANES : (a + 1) * LANES] for a in range(3)]
        w = [weights[at, n * channels + h * LANES : n * channels + (h + 1) * LANES] for n in range(6)]
        return at, s, v, u, w

    def cross(a, b):
        return [a[1] * b[2] - a[2] * b[1], a[2] * b[0] - a[0] * b[2], a[0] * b[1] - a[1] * b[0]]

    def inner(a, b):
        return a[0] * b[0] + a[1] * b[1] + a[2] * b[2]

    for atom in range(atoms):
        coeff[atom : atom + 1, :] = energy_table[pl.ds(species[atom], 1), :]

    cotangents = []
    terms = []
    for h in range(halves):
        lanes = slice(h * LANES, (h + 1) * LANES)
        sums = None
        for step in range(steps):
            at, s, v, u, w = edge_inputs(step, h)
            q = inner(u, v)
            along = w[2] * s + w[5] * q
            keep = w[3] - w[5] * (1.0 / 3.0)
            turned = cross(v, u)
            new = [w[0] * s + w[1] * q] + [along * u[a] + keep * v[a] + w[4] * turned[a] for a in range(3)]
            sums = new if sums is None else [x + y for x, y in zip(sums, new)]
        sums = [x[0:atoms, :] + x[atoms:, :] for x in sums]
        s_out = scalars[:, lanes] + scale * sums[0]
        v_out = [vectors[:, a, lanes] + scale * sums[1 + a] for a in range(3)]
        c = coeff[:, lanes]
        g = gains[:, lanes]
        sig = sigmoid(s_out)
        terms.append(c * s_out * sig + g * inner(v_out, v_out))
        cot_s = readout * c * sig * (1.0 + s_out * (1.0 - sig))
        cot_v = [(2.0 * readout) * g * v_out[a] for a in range(3)]
        cotangents.append([cot_s] + cot_v)
    total = sum(terms[1:], terms[0])
    energies[...] = readout * dot(jnp.ones((8, LANES), f32), total, (1, 1), HIGHEST)[0:1, :]

    for step in range(steps):
        pull = None
        for h in range(halves):
            at, s, v, u, w = edge_inputs(step, h)
            cs, *cv = [scale * jnp.concatenate([x, x], axis=0) for x in cotangents[h]]
            q = inner(u, v)
            along = w[2] * s + w[5] * q
            keep = w[3] - w[5] * (1.0 / 3.0)
            d = inner(cv, u)
            turn = cross(u, cv)
            spin = cross(cv, v)
            both = inner(cv, v)
            dq = cs * w[1] + w[5] * d
            ds = cs * w[0] + w[2] * d
            dv = [dq * u[a] + keep * cv[a] + w[4] * turn[a] for a in range(3)]
            du = [dq * v[a] + along * cv[a] + w[4] * spin[a] for a in range(3)]
            dw = [cs * s, cs * q, s * d, both, inner(u, spin), q * d - both * (1.0 / 3.0)]
            pull = du if pull is None else [x + y for x, y in zip(pull, du)]
            for part, value in enumerate([ds] + dv):
                chunk = part * halves + h
                dfar[at, chunk * LANES : (chunk + 1) * LANES] = value.astype(bf16)
            for n in range(6):
                dweights[at, n * channels + h * LANES : n * channels + (h + 1) * LANES] = dw[n].astype(bf16)
        for a in range(3):
            dsteer[at, a * LANES : (a + 1) * LANES] = pull[a]

    dhidden_two = dot(third[...], dweights[...], (1, 1))
    dpre_two = dhidden_two * usable[...] * sig_two * (1.0 + pre_two * (1.0 - sig_two))
    dhidden_one = dot(second[...], dpre_two.astype(bf16), (1, 0))
    dpre_one = dhidden_one * sig_one * (1.0 + pre_one * (1.0 - sig_one))
    dgauss = dot(first[...], dpre_one.astype(bf16), (1, 0))
    ddistance = jnp.sum(dgauss * gauss * off, axis=0, keepdims=True) * (-2.0 * SHARPNESS)
    ddirection = dot(spread, dsteer[...], (1, 1), HIGHEST)
    radial = jnp.sum(ddirection * direction, axis=0, keepdims=True)
    inv = 1.0 / distance
    dapart = ddirection * inv + (ddistance - radial * inv) * direction
    dapart = jnp.concatenate([dapart, jnp.zeros((LANES - 8, edges), f32)], axis=0)
    dspots = dot(contrast, dapart, (1, 1), HIGHEST)

    def put(chunk, value):
        for which, ref in enumerate(grads):
            first_row = sum(blocks[:which]) * atoms
            for block in range(blocks[which]):
                piece = value[first_row + block * atoms : first_row + (block + 1) * atoms, :]
                at = block * packet + chunk * atoms
                if which == 0 and block == 0:
                    if chunk < chunks:
                        piece = piece + cotangents[chunk % halves][chunk // halves]
                    own_out[chunk * atoms : (chunk + 1) * atoms, :] = piece
                    piece = jnp.zeros_like(piece)
                ref[at : at + atoms, :] = piece

    put(chunks, dspots)
    for chunk in range(chunks):
        put(chunk, dot(picks, dfar[:, chunk * LANES : (chunk + 1) * LANES], (1, 0)))


def finish_kernel(bound_rows, bound_count, own, *rest):
    parts = rest[:-5]
    forces, grad_scalars, grad_vectors, ghost, total = rest[-5:]
    boundary = bound_rows.shape[0]
    atoms, channels = grad_scalars.shape
    halves = channels // LANES
    chunks = 4 * halves
    value = parts[0][...]
    for ref in parts[1:]:
        value = value + ref[...]
    ghost[...] = value
    total[...] = own[...]
    for slot in range(boundary):
        atom = bound_rows[slot]
        alive = jnp.where(slot < bound_count[0], 1.0, 0.0).astype(jnp.float32)
        for chunk in range(chunks + 1):
            at = pl.ds(chunk * atoms + atom, 1)
            total[at, :] = total[at, :] + alive * ghost[chunk * boundary + slot : chunk * boundary + slot + 1, :]
    forces[...] = -total[chunks * atoms :, 0:3]
    for h in range(halves):
        lanes = slice(h * LANES, (h + 1) * LANES)
        grad_scalars[:, lanes] = total[h * atoms : (h + 1) * atoms, :]
        for a in range(3):
            chunk = (1 + a) * halves + h
            grad_vectors[:, a, lanes] = total[chunk * atoms : (chunk + 1) * atoms, :]


VMEM = pl.BlockSpec(memory_space=pltpu.VMEM)
SMEM = pl.BlockSpec(memory_space=pltpu.SMEM)


def shards(
    places, scalars, vectors, species, bound_rows, bound_count, neighbour_ids, neighbour_count,
    radial_first, radial_second, radial_third, energy_table, vector_gains,
):
    f32 = jnp.float32
    atoms, channels = scalars.shape
    boundary = bound_rows.shape[0]
    slots = neighbour_ids.shape[0]
    edges = slots * atoms
    halves = channels // LANES
    chunks = 4 * halves
    packet_rows = (chunks + 1) * boundary

    packet = pl.pallas_call(
        pack_kernel,
        out_shape=jax.ShapeDtypeStruct((packet_rows, LANES), f32),
        in_specs=[SMEM, SMEM, VMEM, VMEM, VMEM],
        out_specs=VMEM,
        name="pack",
    )(bound_rows, bound_count, places, scalars, vectors)

    perms = {axis: sides(lax.axis_size(axis)) for axis in AXES}
    plane = packet
    for axis in ("gx", "gy"):
        plane = jnp.concatenate([plane] + [swap(plane, axis, pairs) for pairs in perms[axis]], axis=0)
    tables = [plane] + [swap(plane, "gz", pairs) for pairs in perms["gz"]]
    wide = {axis: 1 + len(perms[axis]) for axis in AXES}
    per_plane = wide["gx"] * wide["gy"]

    ids = neighbour_ids.reshape(1, edges)
    ghost = ids - atoms
    block, slot = ghost // boundary, ghost % boundary
    offsets = [block // 9 - 1, (block // 3) % 3 - 1, block % 3 - 1]
    slot_at = [slot_of(offset, axis) for offset, axis in zip(offsets, AXES)]
    stored = (slot_at[2] * wide["gy"] + slot_at[1]) * wide["gx"] + slot_at[0]
    row_of = jnp.where(ids < atoms, ids, stored * boundary + slot)
    displace = jnp.concatenate(
        [jnp.where(ids < atoms, 0, offset).astype(f32) * EDGE for offset in offsets]
        + [jnp.zeros((5, edges), f32)],
        axis=0,
    )
    usable = (jnp.arange(slots)[:, None] < neighbour_count[None, :]).astype(f32).reshape(1, edges)

    rows = len(tables) * per_plane * boundary
    geometry = (atoms, slots, channels, (per_plane,) * len(tables), len(tables))
    out = pl.pallas_call(
        functools.partial(core_kernel, geometry),
        out_shape=[
            jax.ShapeDtypeStruct((1, atoms), f32),
            jax.ShapeDtypeStruct(((chunks + 1) * atoms, LANES), f32),
        ]
        + [jax.ShapeDtypeStruct(t.shape, f32) for t in tables],
        in_specs=[SMEM] + [VMEM] * (11 + len(tables)),
        out_specs=[VMEM] * (2 + len(tables)),
        scratch_shapes=[
            pltpu.VMEM((rows, chunks * LANES), jnp.bfloat16),
            pltpu.VMEM((edges, 6 * channels), f32),
            pltpu.VMEM((edges, chunks * LANES), f32),
            pltpu.VMEM((edges, 3 * LANES), f32),
            pltpu.VMEM((atoms, channels), f32),
            pltpu.VMEM((atoms, LANES), f32),
            pltpu.VMEM((edges, chunks * LANES), jnp.bfloat16),
            pltpu.VMEM((edges, 6 * channels), jnp.bfloat16),
            pltpu.VMEM((edges, 3 * LANES), f32),
        ],
        name="edges",
    )(
        species, row_of, displace, usable, places, scalars, vectors,
        radial_first, radial_second, radial_third, energy_table, vector_gains.reshape(1, channels),
        *tables,
    )
    energies, own, *grads = out

    plane = grads[0]
    for pairs, value in zip(perms["gz"], grads[1:]):
        plane = plane + swap(value, "gz", inverse(pairs))
    step = wide["gx"] * packet_rows
    line = plane[:step]
    for n, pairs in enumerate(perms["gy"]):
        line = line + swap(plane[(n + 1) * step : (n + 2) * step], "gy", inverse(pairs))
    parts = [line[:packet_rows]]
    for n, pairs in enumerate(perms["gx"]):
        parts.append(swap(line[(n + 1) * packet_rows : (n + 2) * packet_rows], "gx", inverse(pairs)))

    forces, grad_scalars, grad_vectors = pl.pallas_call(
        finish_kernel,
        out_shape=[
            jax.ShapeDtypeStruct((atoms, 3), f32),
            jax.ShapeDtypeStruct((atoms, channels), f32),
            jax.ShapeDtypeStruct((atoms, 3, channels), f32),
        ],
        in_specs=[SMEM, SMEM] + [VMEM] * (1 + len(parts)),
        out_specs=[VMEM] * 3,
        scratch_shapes=[
            pltpu.VMEM((packet_rows, LANES), f32),
            pltpu.VMEM(((chunks + 1) * atoms, LANES), f32),
        ],
        name="finish",
    )(bound_rows, bound_count, own, *parts)
    return energies.reshape(atoms), forces, grad_scalars, grad_vectors


def solution(mesh):
    every = AXES
    in_specs = (
        P(every, None), P(every, None), P(every, None, None), P(every), P(every), P(every),
        P(None, every), P(every), P(), P(), P(), P(), P(),
    )
    out_specs = (P(every), P(every, None), P(every, None), P(every, None, None))
    return jax.shard_map(shards, mesh=mesh, in_specs=in_specs, out_specs=out_specs, check_vma=False)
```

```python
import functools

import jax
import jax.numpy as jnp
from jax import lax
from jax.experimental import pallas as pl
from jax.experimental.pallas import tpu as pltpu
from jax.sharding import PartitionSpec as P

SOFTENING = 0.25
SHARPNESS = 2.0
FIRST_CENTRE = 0.5
SPACING = 0.4
EDGE = 1.0
LANES = 128
HIGHEST = lax.Precision.HIGHEST
AXES = ("gx", "gy", "gz")


def dot(a, b, dims, precision=None):
    return lax.dot_general(
        a, b, ((dims[:1], dims[1:]), ((), ())), precision=precision,
        preferred_element_type=jnp.float32,
    )


def sides(size):
    if size == 1:
        return []
    if size == 2:
        return [[(0, 1), (1, 0)]]
    if size % 2:
        return [[((i + 1) % size, i) for i in range(size)], [(i, (i + 1) % size) for i in range(size)]]
    pairs = [[(i, (i + 1) % size) for i in range(first, size, 2)] for first in (0, 1)]
    return [half + [(b, a) for a, b in half] for half in pairs]


def swap(value, axis, pairs):
    return lax.ppermute(value, axis, pairs)


def inverse(pairs):
    return [(b, a) for a, b in pairs]


def pack_kernel(bound_rows_in, bound_count_in, places_in, scalars_in, vectors_in, out,
                bound_rows, bound_count, places, scalars, vectors, sems):
    pairs = [
        (bound_rows_in, bound_rows), (bound_count_in, bound_count), (places_in, places),
        (scalars_in, scalars), (vectors_in, vectors),
    ]
    copies = [pltpu.make_async_copy(a, b, sems.at[n]) for n, (a, b) in enumerate(pairs)]
    for copy in copies:
        copy.start()
    for copy in copies:
        copy.wait()
    boundary = bound_rows.shape[0]
    channels = scalars.shape[1]
    halves = channels // LANES
    source = lax.broadcasted_iota(jnp.int32, (places.shape[1], LANES), 0)
    lane = lax.broadcasted_iota(jnp.int32, (places.shape[1], LANES), 1)
    moved = jnp.zeros(source.shape, jnp.float32)
    for slot in range(boundary):
        atom = bound_rows[slot]
        alive = jnp.where(slot < bound_count[0], 1.0, 0.0).astype(jnp.float32)
        rows = [scalars[pl.ds(atom, 1), :]] + [vectors[a, pl.ds(atom, 1), :] for a in range(3)]
        for part, row in enumerate(rows):
            row = row * alive
            for h in range(halves):
                at = (part * halves + h) * boundary + slot
                out[at : at + 1, :] = row[:, h * LANES : (h + 1) * LANES]
        moved = jnp.where((lane == slot) & (source == atom), alive, moved)
    spots = dot(places[...], moved, (1, 0), HIGHEST)
    out[4 * halves * boundary :, :] = jnp.concatenate([spots, jnp.zeros((boundary - 3, LANES), jnp.float32)], axis=0)


def prep_kernel(wide, parities, ids, counts, picks, contrast, displace, usable):
    atoms, slots = ids.shape
    edges = atoms * slots
    f32 = jnp.float32
    lane = lax.broadcasted_iota(jnp.int32, (atoms, edges), 1)
    mine = lane % atoms == lax.broadcasted_iota(jnp.int32, (atoms, edges), 0)
    slot_lane = lax.broadcasted_iota(jnp.int32, (slots, edges), 1) // atoms
    belongs = (slot_lane == lax.broadcasted_iota(jnp.int32, (slots, edges), 0)).astype(f32)
    spread = dot(ids[...].astype(f32), belongs, (1, 0), HIGHEST)
    where = jnp.sum(jnp.where(mine, spread, 0.0), axis=0, keepdims=True).astype(jnp.int32)
    live = dot(jnp.broadcast_to(counts[...], (8, atoms)).astype(f32), mine.astype(f32), (1, 0), HIGHEST)[0:1, :]
    usable[...] = (slot_lane[0:1, :].astype(f32) < live).astype(f32)
    owned = where < atoms
    ghost = jnp.maximum(where - atoms, 0)
    block = ghost // atoms
    offsets = [block // 9 - 1, (block // 3) % 3 - 1, block % 3 - 1]
    stored = jnp.zeros_like(block)
    for axis in (2, 1, 0):
        size, offset = wide[axis], offsets[axis]
        if size == 1:
            at = jnp.zeros_like(offset)
        elif size == 2:
            at = jnp.abs(offset)
        else:
            at = jnp.where(offset == 0, 0, jnp.where(offset == 1 - 2 * parities[axis], 1, 2))
        stored = stored * size + at
    row_of = jnp.where(owned, where, stored * atoms + ghost % atoms)
    row_index = lax.broadcasted_iota(jnp.int32, contrast.shape, 0)
    centre = lax.broadcasted_iota(jnp.int32, contrast.shape, 1) % atoms
    chosen = (row_index == row_of).astype(f32)
    picks[...] = chosen.astype(jnp.bfloat16)
    contrast[...] = chosen - (row_index == centre).astype(f32)
    shift = [jnp.where(owned, 0, offset).astype(f32) * EDGE for offset in offsets]
    displace[...] = jnp.concatenate(shift + [jnp.zeros((5, edges), f32)], axis=0)


def sigmoid(x):
    return 1.0 / (1.0 + jnp.exp(-x))


def core_kernel(
    geometry,
    species, picks_in, contrast_in, displace, usable, places, scalars, vectors, first, second, third,
    energy_table, gains, *rest,
):
    atoms, slots, channels, blocks, tables = geometry
    ghosts = rest[:tables]
    energies, own_out = rest[tables : tables + 2]
    grads = rest[tables + 2 : 2 * tables + 2]
    table, weights, far, steer, coeff, place_rows, dfar, dweights, dsteer = rest[2 * tables + 2 :]
    halves = channels // LANES
    chunks = 4 * halves
    edges = atoms * slots
    packet = (chunks + 1) * atoms
    scale = slots ** (-0.5)
    readout = channels ** (-0.25)
    rows = sum(blocks) * atoms
    f32, bf16 = jnp.float32, jnp.bfloat16

    def pieces(chunk, own):
        parts = []
        for which, ref in enumerate(ghosts):
            for block in range(blocks[which]):
                if which == 0 and block == 0:
                    parts.append(own)
                else:
                    at = block * packet + chunk * atoms
                    parts.append(ref[at : at + atoms, :])
        return jnp.concatenate(parts, axis=0)

    picks, contrast = picks_in[...], contrast_in[...]

    row = 0
    for which, ref in enumerate(ghosts):
        for block in range(blocks[which]):
            at = block * packet + chunks * atoms
            if row:
                place_rows[:, row : row + atoms] = ref[at : at + atoms, 0:atoms]
            else:
                place_rows[0:3, 0:atoms] = places[...]
                place_rows[3:, 0:atoms] = jnp.zeros((atoms - 3, atoms), f32)
            row += atoms
    apart = dot(place_rows[...], contrast, (1, 0), HIGHEST) + displace[...]
    distance = jnp.sqrt(jnp.sum(apart * apart, axis=0, keepdims=True) + SOFTENING)
    direction = apart / distance
    centres = FIRST_CENTRE + SPACING * lax.broadcasted_iota(jnp.int32, (first.shape[0], edges), 0).astype(f32)
    off = distance - centres
    gauss = jnp.exp(-SHARPNESS * off * off)
    pre_one = dot(first[...], gauss.astype(bf16), (0, 0))
    sig_one = sigmoid(pre_one)
    hidden_one = (pre_one * sig_one).astype(bf16)
    pre_two = dot(second[...], hidden_one, (0, 0))
    sig_two = sigmoid(pre_two)
    hidden_two = (pre_two * sig_two * usable[...]).astype(bf16)
    weights[...] = dot(hidden_two, third[...], (0, 0))
    spread = (
        lax.broadcasted_iota(jnp.int32, (8, 3 * LANES), 1) // LANES
        == lax.broadcasted_iota(jnp.int32, (8, 3 * LANES), 0)
    ).astype(f32)
    steer[...] = dot(direction, spread, (0, 0), HIGHEST)

    for part in range(4):
        for h in range(halves):
            chunk = part * halves + h
            lanes = slice(h * LANES, (h + 1) * LANES)
            own = scalars[:, lanes] if part == 0 else vectors[part - 1, :, lanes]
            table[:, chunk * LANES : (chunk + 1) * LANES] = pieces(chunk, own).astype(bf16)
    far[...] = dot(picks, table[...], (0, 0))

    tile = 2 * atoms
    steps = edges // tile

    def edge_inputs(step, h):
        at = slice(step * tile, (step + 1) * tile)
        s = far[at, h * LANES : (h + 1) * LANES]
        v = [far[at, ((1 + a) * halves + h) * LANES : ((1 + a) * halves + h + 1) * LANES] for a in range(3)]
        u = [steer[at, a * LANES : (a + 1) * LANES] for a in range(3)]
        w = [weights[at, n * channels + h * LANES : n * channels + (h + 1) * LANES] for n in range(6)]
        return at, s, v, u, w

    def cross(a, b):
        return [a[1] * b[2] - a[2] * b[1], a[2] * b[0] - a[0] * b[2], a[0] * b[1] - a[1] * b[0]]

    def inner(a, b):
        return a[0] * b[0] + a[1] * b[1] + a[2] * b[2]

    for atom in range(atoms):
        coeff[atom : atom + 1, :] = energy_table[pl.ds(species[atom], 1), :]

    cotangents = []
    terms = []
    for h in range(halves):
        lanes = slice(h * LANES, (h + 1) * LANES)
        sums = None
        for step in range(steps):
            at, s, v, u, w = edge_inputs(step, h)
            q = inner(u, v)
            along = w[2] * s + w[5] * q
            keep = w[3] - w[5] * (1.0 / 3.0)
            turned = cross(v, u)
            new = [w[0] * s + w[1] * q] + [along * u[a] + keep * v[a] + w[4] * turned[a] for a in range(3)]
            sums = new if sums is None else [x + y for x, y in zip(sums, new)]
        sums = [x[0:atoms, :] + x[atoms:, :] for x in sums]
        s_out = scalars[:, lanes] + scale * sums[0]
        v_out = [vectors[a, :, lanes] + scale * sums[1 + a] for a in range(3)]
        c = coeff[:, lanes]
        g = gains[:, lanes]
        sig = sigmoid(s_out)
        terms.append(c * s_out * sig + g * inner(v_out, v_out))
        cot_s = readout * c * sig * (1.0 + s_out * (1.0 - sig))
        cot_v = [(2.0 * readout) * g * v_out[a] for a in range(3)]
        cotangents.append([cot_s] + cot_v)
    total = sum(terms[1:], terms[0])
    energies[...] = readout * dot(jnp.ones((8, LANES), f32), total, (1, 1), HIGHEST)[0:1, :]

    for step in range(steps):
        pull = None
        for h in range(halves):
            at, s, v, u, w = edge_inputs(step, h)
            cs, *cv = [scale * jnp.concatenate([x, x], axis=0) for x in cotangents[h]]
            q = inner(u, v)
            along = w[2] * s + w[5] * q
            keep = w[3] - w[5] * (1.0 / 3.0)
            d = inner(cv, u)
            turn = cross(u, cv)
            spin = cross(cv, v)
            both = inner(cv, v)
            dq = cs * w[1] + w[5] * d
            ds = cs * w[0] + w[2] * d
            dv = [dq * u[a] + keep * cv[a] + w[4] * turn[a] for a in range(3)]
            du = [dq * v[a] + along * cv[a] + w[4] * spin[a] for a in range(3)]
            dw = [cs * s, cs * q, s * d, both, inner(u, spin), q * d - both * (1.0 / 3.0)]
            pull = du if pull is None else [x + y for x, y in zip(pull, du)]
            for part, value in enumerate([ds] + dv):
                chunk = part * halves + h
                dfar[at, chunk * LANES : (chunk + 1) * LANES] = value.astype(bf16)
            for n in range(6):
                dweights[at, n * channels + h * LANES : n * channels + (h + 1) * LANES] = dw[n].astype(bf16)
        for a in range(3):
            dsteer[at, a * LANES : (a + 1) * LANES] = pull[a]

    dhidden_two = dot(third[...], dweights[...], (1, 1))
    dpre_two = dhidden_two * usable[...] * sig_two * (1.0 + pre_two * (1.0 - sig_two))
    dhidden_one = dot(second[...], dpre_two.astype(bf16), (1, 0))
    dpre_one = dhidden_one * sig_one * (1.0 + pre_one * (1.0 - sig_one))
    dgauss = dot(first[...], dpre_one.astype(bf16), (1, 0))
    ddistance = jnp.sum(dgauss * gauss * off, axis=0, keepdims=True) * (-2.0 * SHARPNESS)
    ddirection = dot(spread, dsteer[...], (1, 1), HIGHEST)
    radial = jnp.sum(ddirection * direction, axis=0, keepdims=True)
    inv = 1.0 / distance
    dapart = ddirection * inv + (ddistance - radial * inv) * direction
    dspots = dot(dapart, contrast, (1, 1), HIGHEST)

    def put(chunk, value):
        for which, ref in enumerate(grads):
            first_row = sum(blocks[:which]) * atoms
            for block in range(blocks[which]):
                piece = value[first_row + block * atoms : first_row + (block + 1) * atoms, :]
                at = block * packet + chunk * atoms
                if which == 0 and block == 0:
                    piece = piece + cotangents[chunk % halves][chunk // halves]
                    own_out[chunk * atoms : (chunk + 1) * atoms, :] = piece
                    piece = jnp.zeros_like(piece)
                ref[at : at + atoms, :] = piece

    row = 0
    for which, ref in enumerate(grads):
        for block in range(blocks[which]):
            at = block * packet + chunks * atoms
            piece = dspots[:, row : row + atoms]
            if row == 0:
                own_out[at : at + atoms, :] = jnp.zeros((atoms, LANES), f32)
                own_out[at : at + atoms, 0:atoms] = piece
                piece = jnp.zeros_like(piece)
            ref[at : at + atoms, :] = jnp.zeros((atoms, LANES), f32)
            ref[at : at + atoms, 0:atoms] = piece
            row += atoms
    for chunk in range(chunks):
        put(chunk, dot(picks, dfar[:, chunk * LANES : (chunk + 1) * LANES], (1, 0)))


def finish_kernel(bound_rows, bound_count, energies_in, own, *rest):
    parts = rest[:-6]
    energies, forces, grad_scalars, grad_vectors, ghost, moved = rest[-6:]
    energies[...] = energies_in[...]
    boundary = bound_rows.shape[0]
    atoms, channels = grad_scalars.shape
    halves = channels // LANES
    chunks = 4 * halves
    value = parts[0][...]
    for ref in parts[1:]:
        value = value + ref[...]
    ghost[...] = value
    moved[...] = jnp.zeros(moved.shape, jnp.float32)
    target = lax.broadcasted_iota(jnp.int32, (atoms, LANES), 0)
    lane = lax.broadcasted_iota(jnp.int32, (atoms, LANES), 1)
    lands = jnp.zeros((atoms, LANES), jnp.float32)
    for slot in range(boundary):
        atom = bound_rows[slot]
        alive = jnp.where(slot < bound_count[0], 1.0, 0.0).astype(jnp.float32)
        lands = jnp.where((target == atom) & (lane == slot), alive, lands)
        moved[pl.ds(atom, chunks, stride=atoms), :] = alive * ghost[pl.ds(slot, chunks, stride=boundary), :]
    at = slice(chunks * atoms, (chunks + 1) * atoms)
    forces[...] = -(own[at, 0:atoms] + dot(ghost[at, :], lands, (1, 1), HIGHEST))[0:3, :]
    for h in range(halves):
        lanes = slice(h * LANES, (h + 1) * LANES)
        for part in range(4):
            chunk = part * halves + h
            rows = slice(chunk * atoms, (chunk + 1) * atoms)
            sums = own[rows, :] + moved[rows, :]
            if part == 0:
                grad_scalars[:, lanes] = sums
            else:
                grad_vectors[part - 1, :, lanes] = sums


VMEM = pl.BlockSpec(memory_space=pltpu.VMEM)
SMEM = pl.BlockSpec(memory_space=pltpu.SMEM)


def shards(
    places, scalars, vectors, species, bound_rows, bound_count, neighbour_ids, neighbour_count,
    radial_first, radial_second, radial_third, energy_table, vector_gains,
):
    f32 = jnp.float32
    atoms, channels = scalars.shape
    places, vectors = places.T, vectors.transpose(1, 0, 2)
    boundary = bound_rows.shape[0]
    assert boundary == atoms == 8
    slots = neighbour_ids.shape[0]
    edges = slots * atoms
    halves = channels // LANES
    chunks = 4 * halves
    packet_rows = (chunks + 1) * boundary

    packet = pl.pallas_call(
        pack_kernel,
        out_shape=jax.ShapeDtypeStruct((packet_rows, LANES), f32),
        in_specs=[pl.BlockSpec(memory_space=pltpu.HBM)] * 5,
        out_specs=VMEM,
        scratch_shapes=[
            pltpu.SMEM(bound_rows.shape, jnp.int32),
            pltpu.SMEM(bound_count.shape, jnp.int32),
            pltpu.VMEM(places.shape, f32),
            pltpu.VMEM(scalars.shape, f32),
            pltpu.VMEM(vectors.shape, f32),
            pltpu.SemaphoreType.DMA((5,)),
        ],
        compiler_params=pltpu.CompilerParams(vmem_limit_bytes=2 << 20),
        name="pack",
    )(bound_rows, bound_count, places, scalars, vectors)

    perms = {axis: sides(lax.axis_size(axis)) for axis in AXES}
    wide = {axis: 1 + len(perms[axis]) for axis in AXES}
    per_plane = wide["gx"] * wide["gy"]
    rows = per_plane * wide["gz"] * atoms
    parities = jnp.stack([lax.axis_index(a) % 2 if lax.axis_size(a) % 2 == 0 else 0 for a in AXES])
    prepared = pl.pallas_call(
        functools.partial(prep_kernel, tuple(wide[a] for a in AXES)),
        out_shape=[
            jax.ShapeDtypeStruct((rows, edges), jnp.bfloat16),
            jax.ShapeDtypeStruct((rows, edges), f32),
            jax.ShapeDtypeStruct((8, edges), f32),
            jax.ShapeDtypeStruct((1, edges), f32),
        ],
        in_specs=[SMEM, VMEM, VMEM],
        out_specs=[VMEM] * 4,
        compiler_params=pltpu.CompilerParams(vmem_limit_bytes=2 << 20),
        name="prep",
    )(parities, neighbour_ids.T, neighbour_count.reshape(1, atoms))

    plane = jnp.concatenate([packet] + [swap(packet, "gx", pairs) for pairs in perms["gx"]], axis=0)
    plane, prepared = lax.optimization_barrier((plane, prepared))
    plane = jnp.concatenate([plane] + [swap(plane, "gy", pairs) for pairs in perms["gy"]], axis=0)
    tables = [plane] + [swap(plane, "gz", pairs) for pairs in perms["gz"]]

    geometry = (atoms, slots, channels, (per_plane,) * len(tables), len(tables))
    out = pl.pallas_call(
        functools.partial(core_kernel, geometry),
        out_shape=[
            jax.ShapeDtypeStruct((1, atoms), f32),
            jax.ShapeDtypeStruct(((chunks + 1) * atoms, LANES), f32),
        ]
        + [jax.ShapeDtypeStruct(t.shape, f32) for t in tables],
        in_specs=[SMEM] + [VMEM] * (12 + len(tables)),
        out_specs=[VMEM] * (2 + len(tables)),
        scratch_shapes=[
            pltpu.VMEM((rows, chunks * LANES), jnp.bfloat16),
            pltpu.VMEM((edges, 6 * channels), f32),
            pltpu.VMEM((edges, chunks * LANES), f32),
            pltpu.VMEM((edges, 3 * LANES), f32),
            pltpu.VMEM((atoms, channels), f32),
            pltpu.VMEM((atoms, rows), f32),
            pltpu.VMEM((edges, chunks * LANES), jnp.bfloat16),
            pltpu.VMEM((edges, 6 * channels), jnp.bfloat16),
            pltpu.VMEM((edges, 3 * LANES), f32),
        ],
        compiler_params=pltpu.CompilerParams(vmem_limit_bytes=16 << 20),
        name="edges",
    )(
        species, *prepared, places, scalars, vectors,
        radial_first, radial_second, radial_third, energy_table, vector_gains.reshape(1, channels),
        *tables,
    )
    energies, own, *grads = out

    plane = grads[0]
    for pairs, value in zip(perms["gz"], grads[1:]):
        plane = plane + swap(value, "gz", inverse(pairs))
    step = wide["gx"] * packet_rows
    line = plane[:step]
    for n, pairs in enumerate(perms["gy"]):
        line = line + swap(plane[(n + 1) * step : (n + 2) * step], "gy", inverse(pairs))
    parts = [line[:packet_rows]]
    for n, pairs in enumerate(perms["gx"]):
        parts.append(swap(line[(n + 1) * packet_rows : (n + 2) * packet_rows], "gx", inverse(pairs)))

    energies, forces, grad_scalars, grad_vectors = pl.pallas_call(
        finish_kernel,
        out_shape=[
            jax.ShapeDtypeStruct((1, atoms), f32),
            jax.ShapeDtypeStruct((3, atoms), f32),
            jax.ShapeDtypeStruct((atoms, channels), f32),
            jax.ShapeDtypeStruct((3, atoms, channels), f32),
        ],
        in_specs=[SMEM, SMEM] + [VMEM] * (2 + len(parts)),
        out_specs=[VMEM] * 4,
        scratch_shapes=[
            pltpu.VMEM((packet_rows, LANES), f32),
            pltpu.VMEM((chunks * atoms, LANES), f32),
        ],
        compiler_params=pltpu.CompilerParams(vmem_limit_bytes=2 << 20),
        name="finish",
    )(bound_rows, bound_count, energies, own, *parts)
    return energies.reshape(atoms), forces.T, grad_scalars, grad_vectors.transpose(1, 0, 2)


def solution(mesh):
    every = AXES
    in_specs = (
        P(every, None), P(every, None), P(every, None, None), P(every), P(every), P(every),
        P(None, every), P(every), P(), P(), P(), P(), P(),
    )
    out_specs = (P(every), P(every, None), P(every, None), P(every, None, None))
    return jax.shard_map(shards, mesh=mesh, in_specs=in_specs, out_specs=out_specs, check_vma=False)
```

```python
import functools

import jax
import jax.numpy as jnp
from jax import lax
from jax.experimental import pallas as pl
from jax.experimental.pallas import tpu as pltpu
from jax.sharding import PartitionSpec as P


SOFTENING = 0.25
SHARPNESS = 2.0
FIRST_CENTRE = 0.5
SPACING = 0.4
EDGE = 1.0
LANES = 128
HIGHEST = lax.Precision.HIGHEST
AXES = ("gx", "gy", "gz")


def dot(a, b, dims, precision=None):
    return lax.dot_general(
        a, b, ((dims[:1], dims[1:]), ((), ())), precision=precision,
        preferred_element_type=jnp.float32,
    )


def thirds(x, axis=0):
    high = x.astype(jnp.bfloat16).astype(jnp.float32)
    rest = x - high
    middle = rest.astype(jnp.bfloat16).astype(jnp.float32)
    return jnp.concatenate([high, middle, rest - middle], axis=axis).astype(jnp.bfloat16)


def joined(x, rows):
    return x[0:rows, :] + (x[rows : 2 * rows, :] + x[2 * rows :, :])


def sides(size):
    if size == 1:
        return []
    if size == 2:
        return [[(0, 1), (1, 0)]]
    if size % 2:
        return [[((i + 1) % size, i) for i in range(size)], [(i, (i + 1) % size) for i in range(size)]]
    pairs = [[(i, (i + 1) % size) for i in range(first, size, 2)] for first in (0, 1)]
    return [half + [(b, a) for a, b in half] for half in pairs]


def backwards(pairs_list):
    return reversed(list(enumerate(pairs_list)))


def inverse(pairs):
    return [(b, a) for a, b in pairs]


def pack_kernel(
    bound_count, bound_rows_in, places_in, scalars_in, vectors_in, out,
    bound_rows, places, scalars, vectors, sems,
):
    pairs = [(bound_rows_in, bound_rows), (places_in, places), (scalars_in, scalars), (vectors_in, vectors)]
    copies = [pltpu.make_async_copy(a, b, sems.at[n]) for n, (a, b) in enumerate(pairs)]
    for copy in copies:
        copy.start()
    for copy in copies:
        copy.wait()
    boundary = bound_rows.shape[0]
    channels = scalars.shape[1]
    halves = channels // LANES
    source = lax.broadcasted_iota(jnp.int32, (places.shape[1], LANES), 0)
    lane = lax.broadcasted_iota(jnp.int32, (places.shape[1], LANES), 1)
    moved = jnp.zeros(source.shape, jnp.float32)
    for slot in range(boundary):
        atom = bound_rows[slot]
        alive = jnp.where(slot < bound_count[0], 1.0, 0.0).astype(jnp.float32)
        rows = [scalars[pl.ds(atom, 1), :]] + [vectors[a, pl.ds(atom, 1), :] for a in range(3)]
        for part, row in enumerate(rows):
            row = row * alive
            for h in range(halves):
                at = (part * halves + h) * boundary + slot
                out[at : at + 1, :] = row[:, h * LANES : (h + 1) * LANES]
        moved = jnp.where((lane == slot) & (source == atom), alive, moved)
    spots = dot(places[...], moved, (1, 0), HIGHEST)
    out[4 * halves * boundary :, :] = jnp.concatenate([spots, jnp.zeros((boundary - 3, LANES), jnp.float32)], axis=0)


def prep_kernel(
    wide, parities, ids, counts, species, energy_table, bound_rows, bound_count, *rest
):
    atoms, slots = ids.shape
    edges = atoms * slots
    f32 = jnp.float32
    count = (len(rest) - 6) // 2
    passed, (picks, contrast, displace, usable, coeff, lands), copied = rest[:count], rest[count:-count], rest[-count:]
    for a, b in zip(passed, copied):
        b[...] = a[...]
    lane = lax.broadcasted_iota(jnp.int32, (atoms, edges), 1)
    mine = lane % atoms == lax.broadcasted_iota(jnp.int32, (atoms, edges), 0)
    slot_lane = lax.broadcasted_iota(jnp.int32, (slots, edges), 1) // atoms
    belongs = (slot_lane == lax.broadcasted_iota(jnp.int32, (slots, edges), 0)).astype(f32)
    spread = dot(ids[...].astype(f32), belongs, (1, 0), HIGHEST)
    where = jnp.sum(jnp.where(mine, spread, 0.0), axis=0, keepdims=True).astype(jnp.int32)
    live = dot(jnp.broadcast_to(counts[...], (8, atoms)).astype(f32), mine.astype(f32), (1, 0), HIGHEST)[0:1, :]
    usable[...] = (slot_lane[0:1, :].astype(f32) < live).astype(f32)
    owned = where < atoms
    ghost = jnp.maximum(where - atoms, 0)
    block = ghost // atoms
    offsets = [block // 9 - 1, (block // 3) % 3 - 1, block % 3 - 1]
    at = []
    for axis, offset in enumerate(offsets):
        if wide[axis] == 1:
            at.append(jnp.zeros_like(offset))
        elif wide[axis] == 2:
            at.append(jnp.abs(offset))
        else:
            at.append(jnp.where(offset == 0, 0, jnp.where(offset == 1 - 2 * parities[axis], 1, 2)))
    inside = jnp.where(
        at[1] == 0, at[0],
        jnp.where(at[0] == 0, wide[0] - 1 + at[1], wide[0] + wide[1] - 1 + (at[1] - 1) * (wide[0] - 1) + at[0] - 1),
    )
    stored = at[2] * (wide[0] * wide[1]) + inside
    row_of = jnp.where(owned, where, stored * atoms + ghost % atoms)
    row_index = lax.broadcasted_iota(jnp.int32, contrast.shape, 0)
    centre = lax.broadcasted_iota(jnp.int32, contrast.shape, 1) % atoms
    chosen = (row_index == row_of).astype(f32)
    picks[...] = chosen.astype(jnp.bfloat16)
    contrast[...] = (chosen - (row_index == centre).astype(f32)).astype(jnp.bfloat16)
    kinds = (lax.broadcasted_iota(jnp.int32, (energy_table.shape[0], atoms), 0) == species[...]).astype(f32)
    coeff[...] = dot(kinds, energy_table[...], (0, 0), HIGHEST)
    slot = lax.broadcasted_iota(jnp.int32, (atoms, atoms), 1)
    target = lax.broadcasted_iota(jnp.int32, (atoms, atoms), 0)
    land = ((target == bound_rows[...]) & (slot < bound_count[...])).astype(f32)
    lands[...] = jnp.concatenate([land, land, land], axis=1)
    shift = [jnp.where(owned, 0, offset).astype(f32) * EDGE for offset in offsets]
    displace[...] = jnp.concatenate(shift + [jnp.zeros((5, edges), f32)], axis=0)


def sigmoid(x):
    return 1.0 / (1.0 + jnp.exp(-x))


def core_kernel(
    geometry,
    picks_in, contrast_in, displace, usable, coeff, places, scalars, vectors, first, second, third,
    gains, *rest,
):
    atoms, slots, channels, blocks, sinks, order = geometry
    tables = len(blocks)
    ghosts = rest[:tables]
    energies, own_out = rest[tables : tables + 2]
    grads = rest[tables + 2 : tables + 2 + len(sinks)]
    table, weights, far, steer, messages, place_rows, dfar, dweights, dsteer = rest[tables + 2 + len(sinks) :]
    halves = channels // LANES
    chunks = 4 * halves
    edges = atoms * slots
    packet = (chunks + 1) * atoms
    scale = slots ** (-0.5)
    readout = channels ** (-0.25)
    rows = sum(blocks) * atoms
    f32, bf16 = jnp.float32, jnp.bfloat16

    def pieces(chunk, own):
        parts = []
        for which, ref in enumerate(ghosts):
            for block in range(blocks[which]):
                if which == 0 and block == 0:
                    parts.append(own)
                else:
                    at = block * packet + chunk * atoms
                    parts.append(ref[at : at + atoms, :])
        return jnp.concatenate(parts, axis=0)

    picks, contrast = picks_in[...], contrast_in[...]

    row = 0
    for which, ref in enumerate(ghosts):
        for block in range(blocks[which]):
            at = block * packet + chunks * atoms
            if row:
                place_rows[:, row : row + atoms] = ref[at : at + atoms, 0:atoms]
            else:
                place_rows[0:3, 0:atoms] = places[...]
                place_rows[3:, 0:atoms] = jnp.zeros((atoms - 3, atoms), f32)
            row += atoms
    apart = joined(dot(thirds(place_rows[...]), contrast, (1, 0)), 8) + displace[...]
    distance = jnp.sqrt(jnp.sum(apart * apart, axis=0, keepdims=True) + SOFTENING)
    direction = apart / distance
    centres = FIRST_CENTRE + SPACING * lax.broadcasted_iota(jnp.int32, (first.shape[0], edges), 0).astype(f32)
    off = distance - centres
    gauss = jnp.exp(-SHARPNESS * off * off)
    pre_one = dot(first[...], gauss.astype(bf16), (0, 0))
    sig_one = sigmoid(pre_one)
    hidden_one = (pre_one * sig_one).astype(bf16)
    pre_two = dot(second[...], hidden_one, (0, 0))
    sig_two = sigmoid(pre_two)
    hidden_two = (pre_two * sig_two * usable[...]).astype(bf16)
    weights[...] = dot(hidden_two, third[...], (0, 0)).astype(bf16)
    spread = (
        lax.broadcasted_iota(jnp.int32, (8, 3 * LANES), 1) // LANES
        == lax.broadcasted_iota(jnp.int32, (8, 3 * LANES), 0)
    ).astype(f32).astype(bf16)
    steer[...] = dot(direction.astype(bf16), spread, (0, 0)).astype(bf16)

    for part in range(4):
        for h in range(halves):
            chunk = part * halves + h
            lanes = slice(h * LANES, (h + 1) * LANES)
            own = scalars[:, lanes] if part == 0 else vectors[part - 1, :, lanes]
            table[:, chunk * LANES : (chunk + 1) * LANES] = pieces(chunk, own).astype(bf16)
    far[...] = dot(picks, table[...], (0, 0)).astype(bf16)

    tile = 2 * atoms
    steps = edges // tile
    third_part = jnp.asarray(1.0 / 3.0, bf16)

    def edge_inputs(step, h):
        at = slice(step * tile, (step + 1) * tile)
        s = far[at, h * LANES : (h + 1) * LANES]
        v = [far[at, ((1 + a) * halves + h) * LANES : ((1 + a) * halves + h + 1) * LANES] for a in range(3)]
        u = [steer[at, a * LANES : (a + 1) * LANES] for a in range(3)]
        w = [weights[at, n * channels + h * LANES : n * channels + (h + 1) * LANES] for n in range(6)]
        return at, s, v, u, w

    def cross(a, b):
        return [a[1] * b[2] - a[2] * b[1], a[2] * b[0] - a[0] * b[2], a[0] * b[1] - a[1] * b[0]]

    def inner(a, b):
        return a[0] * b[0] + a[1] * b[1] + a[2] * b[2]

    for step in range(steps):
        for h in range(halves):
            at, s, v, u, w = edge_inputs(step, h)
            q = inner(u, v)
            along = w[2] * s + w[5] * q
            keep = w[3] - w[5] * third_part
            turned = cross([w[4] * x for x in v], u)
            new = [w[0] * s + w[1] * q] + [along * u[a] + keep * v[a] + turned[a] for a in range(3)]
            for part, value in enumerate(new):
                chunk = part * halves + h
                messages[at, chunk * LANES : (chunk + 1) * LANES] = value
    centre = lax.broadcasted_iota(jnp.int32, (atoms, edges), 1) % atoms
    mine = (centre == lax.broadcasted_iota(jnp.int32, (atoms, edges), 0)).astype(f32).astype(bf16)
    summed = dot(mine, messages[...], (1, 0))

    cotangents = []
    terms = []
    for h in range(halves):
        lanes = slice(h * LANES, (h + 1) * LANES)
        sums = [summed[:, (p * halves + h) * LANES : (p * halves + h + 1) * LANES] for p in range(4)]
        s_out = scalars[:, lanes] + scale * sums[0]
        v_out = [vectors[a, :, lanes] + scale * sums[1 + a] for a in range(3)]
        c = coeff[:, lanes]
        g = gains[:, lanes]
        sig = sigmoid(s_out)
        terms.append(c * s_out * sig + g * inner(v_out, v_out))
        cot_s = readout * c * sig * (1.0 + s_out * (1.0 - sig))
        cot_v = [(2.0 * readout) * g * v_out[a] for a in range(3)]
        cotangents.append([cot_s] + cot_v)
    total = sum(terms[1:], terms[0])
    energies[...] = readout * dot(jnp.ones((8, LANES), f32), total, (1, 1), HIGHEST)[0:1, :]

    pulled = [[(scale * jnp.concatenate([x, x], axis=0)).astype(bf16) for x in c] for c in cotangents]
    for step in range(steps):
        for h in range(halves):
            at, s, v, u, w = edge_inputs(step, h)
            cs, *cv = pulled[h]
            q = inner(u, v)
            along = w[2] * s + w[5] * q
            keep = w[3] - w[5] * third_part
            d = inner(cv, u)
            turn = cross(u, cv)
            spin = cross(cv, v)
            both = inner(cv, v)
            dq = cs * w[1] + w[5] * d
            ds = cs * w[0] + w[2] * d
            dv = [dq * u[a] + keep * cv[a] + w[4] * turn[a] for a in range(3)]
            du = [dq * v[a] + along * cv[a] + w[4] * spin[a] for a in range(3)]
            dw = [cs * s, cs * q, s * d, both, inner(u, spin), q * d - both * third_part]
            for part, value in enumerate([ds] + dv):
                chunk = part * halves + h
                dfar[at, chunk * LANES : (chunk + 1) * LANES] = value
            for n in range(6):
                dweights[at, n * channels + h * LANES : n * channels + (h + 1) * LANES] = dw[n]
            for a in range(3):
                dsteer[at, (a * halves + h) * LANES : (a * halves + h + 1) * LANES] = du[a]

    def put(chunk, value):
        for which, ref in enumerate(grads):
            for block in range(sinks[which]):
                row = (which * len(order) + order[block]) * atoms
                piece = value[row : row + atoms, :]
                at = block * packet + chunk * atoms
                if which == 0 and block == 0:
                    piece = piece + cotangents[chunk % halves][chunk // halves]
                    own_out[chunk * atoms : (chunk + 1) * atoms, :] = piece
                    piece = jnp.zeros_like(piece)
                ref[at : at + atoms, :] = piece

    for chunk in range(chunks):
        put(chunk, dot(picks, dfar[:, chunk * LANES : (chunk + 1) * LANES], (1, 0)))

    dhidden_two = dot(third[...], dweights[...], (1, 1))
    dpre_two = dhidden_two * usable[...] * sig_two * (1.0 + pre_two * (1.0 - sig_two))
    dhidden_one = dot(second[...], dpre_two.astype(bf16), (1, 0))
    dpre_one = dhidden_one * sig_one * (1.0 + pre_one * (1.0 - sig_one))
    dgauss = dot(first[...], dpre_one.astype(bf16), (1, 0))
    ddistance = jnp.sum(dgauss * gauss * off, axis=0, keepdims=True) * (-2.0 * SHARPNESS)
    gather = (
        lax.broadcasted_iota(jnp.int32, (8, 3 * channels), 1) // channels
        == lax.broadcasted_iota(jnp.int32, (8, 3 * channels), 0)
    ).astype(f32).astype(bf16)
    ddirection = dot(gather, dsteer[...], (1, 1))
    radial = jnp.sum(ddirection * direction, axis=0, keepdims=True)
    inv = 1.0 / distance
    dapart = ddirection * inv + (ddistance - radial * inv) * direction
    dspots = joined(dot(thirds(dapart), contrast, (1, 1)), 8)

    for which, ref in enumerate(grads):
        for block in range(sinks[which]):
            at = block * packet + chunks * atoms
            row = (which * len(order) + order[block]) * atoms
            piece = dspots[:, row : row + atoms]
            if row == 0:
                own_out[at : at + atoms, :] = jnp.zeros((atoms, LANES), f32)
                own_out[at : at + atoms, 0:atoms] = piece
                piece = jnp.zeros_like(piece)
            ref[at : at + atoms, :] = jnp.zeros((atoms, LANES), f32)
            ref[at : at + atoms, 0:atoms] = piece


def finish_kernel(energies_in, own, lands, *rest):
    parts = rest[:-8]
    energies, forces, grad_scalars, grad_vectors, moved, scalar_rows, vector_rows, sems = rest[-8:]
    atoms, channels = scalar_rows.shape
    halves = channels // LANES
    chunks = 4 * halves
    copies = [
        pltpu.make_async_copy(a, b, sems.at[n])
        for n, (a, b) in enumerate([
            (energies_in, energies), (moved, forces), (scalar_rows, grad_scalars), (vector_rows, grad_vectors),
        ])
    ]
    copies[0].start()
    value = parts[0][...]
    for ref in parts[1:]:
        value = value + ref[...]
    ghost = [value[c * atoms : (c + 1) * atoms, :] for c in range(chunks + 1)]
    land = lands[...].astype(jnp.bfloat16)
    sums = dot(land, thirds(jnp.concatenate(ghost[:chunks], axis=1)), (1, 0))
    for part in (1, 2, 3, 0):
        for h in range(halves):
            chunk = part * halves + h
            total = own[chunk * atoms : (chunk + 1) * atoms, :] + sums[:, chunk * LANES : (chunk + 1) * LANES]
            lanes = slice(h * LANES, (h + 1) * LANES)
            if part:
                vector_rows[part - 1, :, lanes] = total
            else:
                scalar_rows[:, lanes] = total
        if part == 3:
            copies[3].start()
    copies[2].start()
    spots = joined(dot(thirds(ghost[chunks][:, 0:atoms]), land[:, 0:atoms], (1, 1)), atoms)
    moved[...] = -(own[chunks * atoms :, 0:atoms] + spots)[0:3, :]
    copies[1].start()
    for copy in copies:
        copy.wait()


VMEM = pl.BlockSpec(memory_space=pltpu.VMEM)
SMEM = pl.BlockSpec(memory_space=pltpu.SMEM)


def shards(
    places, scalars, vectors, species, bound_rows, bound_count, neighbour_ids, neighbour_count,
    radial_first, radial_second, radial_third, energy_table, vector_gains,
):
    f32 = jnp.float32
    atoms, channels = scalars.shape
    places, vectors = places.T, vectors.transpose(1, 0, 2)
    boundary = bound_rows.shape[0]
    assert boundary == atoms == 8
    slots = neighbour_ids.shape[0]
    edges = slots * atoms
    halves = channels // LANES
    chunks = 4 * halves
    packet_rows = (chunks + 1) * boundary

    packet = pl.pallas_call(
        pack_kernel,
        out_shape=jax.ShapeDtypeStruct((packet_rows, LANES), f32),
        in_specs=[SMEM] + [pl.BlockSpec(memory_space=pltpu.HBM)] * 4,
        out_specs=VMEM,
        scratch_shapes=[
            pltpu.SMEM(bound_rows.shape, jnp.int32),
            pltpu.VMEM(places.shape, f32),
            pltpu.VMEM(scalars.shape, f32),
            pltpu.VMEM(vectors.shape, f32),
            pltpu.SemaphoreType.DMA((4,)),
        ],
        compiler_params=pltpu.CompilerParams(vmem_limit_bytes=2 << 20),
        name="pack",
    )(bound_count, *[pltpu.with_memory_space_constraint(x, pltpu.HBM) for x in (bound_rows, places, scalars, vectors)])

    perms = {axis: sides(lax.axis_size(axis)) for axis in AXES}
    wide = {axis: 1 + len(perms[axis]) for axis in AXES}
    per_plane = wide["gx"] * wide["gy"]
    rows = per_plane * wide["gz"] * atoms
    beside_x = [lax.ppermute(packet, "gx", pairs) for pairs in perms["gx"]]
    beside_y = [lax.ppermute(packet, "gy", pairs) for pairs in perms["gy"]]
    across = jnp.concatenate(beside_x, axis=0)
    across, ids, counts = lax.optimization_barrier((across, neighbour_ids.T, neighbour_count.reshape(1, atoms)))
    plain = [
        places, scalars, vectors, radial_first, radial_second, radial_third, vector_gains.reshape(1, channels),
    ]
    parities = jnp.stack([lax.axis_index(a) % 2 if lax.axis_size(a) % 2 == 0 else 0 for a in AXES])
    prepared = pl.pallas_call(
        functools.partial(prep_kernel, tuple(wide[a] for a in AXES)),
        out_shape=[
            jax.ShapeDtypeStruct((rows, edges), jnp.bfloat16),
            jax.ShapeDtypeStruct((rows, edges), jnp.bfloat16),
            jax.ShapeDtypeStruct((8, edges), f32),
            jax.ShapeDtypeStruct((1, edges), f32),
            jax.ShapeDtypeStruct((atoms, channels), f32),
            jax.ShapeDtypeStruct((atoms, 3 * atoms), f32),
        ]
        + [jax.ShapeDtypeStruct(x.shape, x.dtype) for x in plain],
        in_specs=[SMEM] + [VMEM] * (6 + len(plain)),
        out_specs=[VMEM] * (6 + len(plain)),
        compiler_params=pltpu.CompilerParams(vmem_limit_bytes=2 << 20),
        name="prep",
    )(
        parities, ids, counts, species.reshape(1, atoms), energy_table,
        bound_rows.reshape(1, boundary), bound_count.reshape(1, 1), *plain,
    )
    prepared, plain = prepared[:6], prepared[6:]
    *prepared, lands = prepared
    corners = [lax.ppermute(across, "gy", pairs) for pairs in perms["gy"]]
    cross = jnp.concatenate([packet, across] + beside_y, axis=0)
    corner = jnp.concatenate(corners, axis=0)
    tables = [packet, across] + beside_y + corners
    for pairs in perms["gz"]:
        tables += [lax.ppermute(cross, "gz", pairs), lax.ppermute(corner, "gz", pairs)]
    blocks = tuple(t.shape[0] // packet_rows for t in tables)
    sinks = (per_plane,) * wide["gz"]

    nx, ny = wide["gx"], wide["gy"]
    order = [x for x in range(nx)]
    for y in range(1, ny):
        order += [nx + y - 1] + [nx + ny - 1 + (y - 1) * (nx - 1) + x - 1 for x in range(1, nx)]
    geometry = (atoms, slots, channels, blocks, sinks, tuple(order))
    out = pl.pallas_call(
        functools.partial(core_kernel, geometry),
        out_shape=[
            jax.ShapeDtypeStruct((1, atoms), f32),
            jax.ShapeDtypeStruct(((chunks + 1) * atoms, LANES), f32),
        ]
        + [jax.ShapeDtypeStruct((n * packet_rows, LANES), f32) for n in sinks],
        in_specs=[VMEM] * (12 + len(tables)),
        out_specs=[VMEM] * (2 + len(sinks)),
        scratch_shapes=[
            pltpu.VMEM((rows, chunks * LANES), jnp.bfloat16),
            pltpu.VMEM((edges, 6 * channels), jnp.bfloat16),
            pltpu.VMEM((edges, chunks * LANES), jnp.bfloat16),
            pltpu.VMEM((edges, 3 * LANES), jnp.bfloat16),
            pltpu.VMEM((edges, chunks * LANES), jnp.bfloat16),
            pltpu.VMEM((atoms, rows), f32),
            pltpu.VMEM((edges, chunks * LANES), jnp.bfloat16),
            pltpu.VMEM((edges, 6 * channels), jnp.bfloat16),
            pltpu.VMEM((edges, 3 * channels), jnp.bfloat16),
        ],
        compiler_params=pltpu.CompilerParams(vmem_limit_bytes=16 << 20),
        name="edges",
    )(
        *prepared, *plain, *tables,
    )
    energies, own, *grads = out

    plane = grads[0]
    for n, pairs in enumerate(perms["gz"]):
        plane = plane + lax.ppermute(grads[n + 1], "gz", inverse(pairs))
    step = wide["gx"] * packet_rows
    line = plane[:step]
    for n, pairs in backwards(perms["gy"]):
        line = line + lax.ppermute(plane[(n + 1) * step : (n + 2) * step], "gy", inverse(pairs))
    parts = [line[:packet_rows]]
    for n, pairs in backwards(perms["gx"]):
        parts.append(lax.ppermute(line[(n + 1) * packet_rows : (n + 2) * packet_rows], "gx", inverse(pairs)))

    energies, forces, grad_scalars, grad_vectors = pl.pallas_call(
        finish_kernel,
        out_shape=[
            jax.ShapeDtypeStruct((1, atoms), f32),
            jax.ShapeDtypeStruct((3, atoms), f32),
            jax.ShapeDtypeStruct((atoms, channels), f32),
            jax.ShapeDtypeStruct((3, atoms, channels), f32),
        ],
        in_specs=[VMEM] * (3 + len(parts)),
        out_specs=[pl.BlockSpec(memory_space=pltpu.HBM)] * 4,
        scratch_shapes=[
            pltpu.VMEM((3, atoms), f32),
            pltpu.VMEM((atoms, channels), f32),
            pltpu.VMEM((3, atoms, channels), f32),
            pltpu.SemaphoreType.DMA((4,)),
        ],
        compiler_params=pltpu.CompilerParams(vmem_limit_bytes=2 << 20),
        name="finish",
    )(energies, own, lands, *parts)
    return energies.reshape(atoms), forces.T, grad_scalars, grad_vectors.transpose(1, 0, 2)


def solution(mesh):
    every = AXES
    in_specs = (
        P(every, None), P(every, None), P(every, None, None), P(every), P(every), P(every),
        P(None, every), P(every), P(), P(), P(), P(), P(),
    )
    out_specs = (P(every), P(every, None), P(every, None), P(every, None, None))

    return jax.shard_map(shards, mesh=mesh, in_specs=in_specs, out_specs=out_specs, check_vma=False)
```

```python
import functools

import jax
import jax.numpy as jnp
from jax import lax
from jax.experimental import pallas as pl
from jax.experimental.pallas import tpu as pltpu
from jax.sharding import PartitionSpec as P


SOFTENING = 0.25
SHARPNESS = 2.0
FIRST_CENTRE = 0.5
SPACING = 0.4
EDGE = 1.0
LANES = 128
HIGHEST = lax.Precision.HIGHEST
AXES = ("gx", "gy", "gz")


def dot(a, b, dims, precision=None):
    return lax.dot_general(
        a, b, ((dims[:1], dims[1:]), ((), ())), precision=precision,
        preferred_element_type=jnp.float32,
    )


def thirds(x, axis=0):
    high = x.astype(jnp.bfloat16).astype(jnp.float32)
    rest = x - high
    middle = rest.astype(jnp.bfloat16).astype(jnp.float32)
    return jnp.concatenate([high, middle, rest - middle], axis=axis).astype(jnp.bfloat16)


def joined(x, rows):
    return x[0:rows, :] + (x[rows : 2 * rows, :] + x[2 * rows :, :])


def sides(size):
    if size == 1:
        return []
    if size == 2:
        return [[(0, 1), (1, 0)]]
    if size % 2:
        return [[((i + 1) % size, i) for i in range(size)], [(i, (i + 1) % size) for i in range(size)]]
    pairs = [[(i, (i + 1) % size) for i in range(first, size, 2)] for first in (0, 1)]
    return [half + [(b, a) for a, b in half] for half in pairs]


def backwards(pairs_list):
    return reversed(list(enumerate(pairs_list)))


def inverse(pairs):
    return [(b, a) for a, b in pairs]


def pack_kernel(
    bound_count, bound_rows_in, places_in, scalars_in, vectors_in, out,
    bound_rows, places, scalars, vectors, sems,
):
    pairs = [(bound_rows_in, bound_rows), (places_in, places), (scalars_in, scalars), (vectors_in, vectors)]
    copies = [pltpu.make_async_copy(a, b, sems.at[n]) for n, (a, b) in enumerate(pairs)]
    for copy in copies:
        copy.start()
    for copy in copies:
        copy.wait()
    boundary = bound_rows.shape[0]
    channels = scalars.shape[1]
    halves = channels // LANES
    source = lax.broadcasted_iota(jnp.int32, (places.shape[1], LANES), 0)
    lane = lax.broadcasted_iota(jnp.int32, (places.shape[1], LANES), 1)
    moved = jnp.zeros(source.shape, jnp.float32)
    for slot in range(boundary):
        atom = bound_rows[slot]
        alive = jnp.where(slot < bound_count[0], 1.0, 0.0).astype(jnp.float32)
        rows = [scalars[pl.ds(atom, 1), :]] + [vectors[a, pl.ds(atom, 1), :] for a in range(3)]
        for part, row in enumerate(rows):
            row = row * alive
            for h in range(halves):
                at = (part * halves + h) * boundary + slot
                out[at : at + 1, :] = row[:, h * LANES : (h + 1) * LANES]
        moved = jnp.where((lane == slot) & (source == atom), alive, moved)
    spots = dot(places[...], moved, (1, 0), HIGHEST)
    out[4 * halves * boundary :, :] = jnp.concatenate([spots, jnp.zeros((boundary - 3, LANES), jnp.float32)], axis=0)


def prep_kernel(
    wide, parities, ids, counts, species, energy_table, bound_rows, bound_count, *rest
):
    atoms, slots = ids.shape
    edges = atoms * slots
    f32 = jnp.float32
    count = (len(rest) - 6) // 2
    passed, (picks, contrast, displace, usable, coeff, lands), copied = rest[:count], rest[count:-count], rest[-count:]
    for a, b in zip(passed, copied):
        b[...] = a[...]
    lane = lax.broadcasted_iota(jnp.int32, (atoms, edges), 1)
    mine = lane % atoms == lax.broadcasted_iota(jnp.int32, (atoms, edges), 0)
    slot_lane = lax.broadcasted_iota(jnp.int32, (slots, edges), 1) // atoms
    belongs = (slot_lane == lax.broadcasted_iota(jnp.int32, (slots, edges), 0)).astype(f32)
    spread = dot(ids[...].astype(f32), belongs, (1, 0), HIGHEST)
    where = jnp.sum(jnp.where(mine, spread, 0.0), axis=0, keepdims=True).astype(jnp.int32)
    live = dot(jnp.broadcast_to(counts[...], (8, atoms)).astype(f32), mine.astype(f32), (1, 0), HIGHEST)[0:1, :]
    usable[...] = (slot_lane[0:1, :].astype(f32) < live).astype(f32)
    owned = where < atoms
    ghost = jnp.maximum(where - atoms, 0)
    block = ghost // atoms
    offsets = [block // 9 - 1, (block // 3) % 3 - 1, block % 3 - 1]
    at = []
    for axis, offset in enumerate(offsets):
        if wide[axis] == 1:
            at.append(jnp.zeros_like(offset))
        elif wide[axis] == 2:
            at.append(jnp.abs(offset))
        else:
            at.append(jnp.where(offset == 0, 0, jnp.where(offset == 1 - 2 * parities[axis], 1, 2)))
    inside = jnp.where(
        at[1] == 0, at[0],
        jnp.where(at[0] == 0, wide[0] - 1 + at[1], wide[0] + wide[1] - 1 + (at[1] - 1) * (wide[0] - 1) + at[0] - 1),
    )
    stored = at[2] * (wide[0] * wide[1]) + inside
    row_of = jnp.where(owned, where, stored * atoms + ghost % atoms)
    row_index = lax.broadcasted_iota(jnp.int32, contrast.shape, 0)
    centre = lax.broadcasted_iota(jnp.int32, contrast.shape, 1) % atoms
    chosen = (row_index == row_of).astype(f32)
    picks[...] = chosen.astype(jnp.bfloat16)
    contrast[...] = (chosen - (row_index == centre).astype(f32)).astype(jnp.bfloat16)
    kinds = (lax.broadcasted_iota(jnp.int32, (energy_table.shape[0], atoms), 0) == species[...]).astype(f32)
    coeff[...] = dot(kinds, energy_table[...], (0, 0), HIGHEST)
    slot = lax.broadcasted_iota(jnp.int32, (atoms, atoms), 1)
    target = lax.broadcasted_iota(jnp.int32, (atoms, atoms), 0)
    land = ((target == bound_rows[...]) & (slot < bound_count[...])).astype(f32)
    lands[...] = jnp.concatenate([land, land, land], axis=1)
    shift = [jnp.where(owned, 0, offset).astype(f32) * EDGE for offset in offsets]
    displace[...] = jnp.concatenate(shift + [jnp.zeros((5, edges), f32)], axis=0)


def sigmoid(x):
    return 1.0 / (1.0 + jnp.exp(-x))


def core_kernel(
    geometry,
    picks_in, contrast_in, displace, usable, coeff, places, scalars, vectors, first, second, third,
    gains, *rest,
):
    atoms, slots, channels, blocks, sinks = geometry
    tables = len(blocks)
    ghosts = rest[:tables]
    energies, own_out = rest[tables : tables + 2]
    grads = rest[tables + 2 : tables + 2 + len(sinks)]
    table, weights, far, steer, place_rows = rest[tables + 2 + len(sinks) :]
    halves = channels // LANES
    chunks = 4 * halves
    edges = atoms * slots
    packet = (chunks + 1) * atoms
    scale = slots ** (-0.5)
    readout = channels ** (-0.25)
    rows = sum(blocks) * atoms
    f32, bf16 = jnp.float32, jnp.bfloat16

    def pieces(chunk, own):
        parts = []
        for which, ref in enumerate(ghosts):
            for block in range(blocks[which]):
                if which == 0 and block == 0:
                    parts.append(own)
                else:
                    at = block * packet + chunk * atoms
                    parts.append(ref[at : at + atoms, :])
        return jnp.concatenate(parts, axis=0)

    picks, contrast = picks_in[...], contrast_in[...]

    row = 0
    for which, ref in enumerate(ghosts):
        for block in range(blocks[which]):
            at = block * packet + chunks * atoms
            if row:
                place_rows[:, row : row + atoms] = ref[at : at + atoms, 0:atoms]
            else:
                place_rows[0:3, 0:atoms] = places[...]
                place_rows[3:, 0:atoms] = jnp.zeros((atoms - 3, atoms), f32)
            row += atoms
    apart = joined(dot(thirds(place_rows[...]), contrast, (1, 0)), 8) + displace[...]
    distance = jnp.sqrt(jnp.sum(apart * apart, axis=0, keepdims=True) + SOFTENING)
    direction = apart / distance
    centres = FIRST_CENTRE + SPACING * lax.broadcasted_iota(jnp.int32, (first.shape[0], edges), 0).astype(f32)
    off = distance - centres
    gauss = jnp.exp(-SHARPNESS * off * off)
    pre_one = dot(first[...], gauss.astype(bf16), (0, 0))
    sig_one = sigmoid(pre_one)
    hidden_one = (pre_one * sig_one).astype(bf16)
    pre_two = dot(second[...], hidden_one, (0, 0))
    sig_two = sigmoid(pre_two)
    hidden_two = (pre_two * sig_two * usable[...]).astype(bf16)
    weights[...] = dot(hidden_two, third[...], (0, 0))
    spread = (
        lax.broadcasted_iota(jnp.int32, (8, 3 * LANES), 1) // LANES
        == lax.broadcasted_iota(jnp.int32, (8, 3 * LANES), 0)
    ).astype(f32).astype(bf16)
    steer[...] = dot(direction.astype(bf16), spread, (0, 0))

    for part in range(4):
        for h in range(halves):
            chunk = part * halves + h
            lanes = slice(h * LANES, (h + 1) * LANES)
            own = scalars[:, lanes] if part == 0 else vectors[part - 1, :, lanes]
            table[:, chunk * LANES : (chunk + 1) * LANES] = pieces(chunk, own).astype(bf16)
    far[...] = dot(picks, table[...], (0, 0))

    tile = 2 * atoms
    steps = edges // tile
    third_part = jnp.asarray(1.0 / 3.0, bf16)

    def edge_inputs(step, h):
        at = slice(step * tile, (step + 1) * tile)
        s = far[at, h * LANES : (h + 1) * LANES].astype(bf16)
        v = [far[at, ((1 + a) * halves + h) * LANES : ((1 + a) * halves + h + 1) * LANES].astype(bf16) for a in range(3)]
        u = [steer[at, a * LANES : (a + 1) * LANES].astype(bf16) for a in range(3)]
        w = [weights[at, n * channels + h * LANES : n * channels + (h + 1) * LANES].astype(bf16) for n in range(6)]
        return at, s, v, u, w

    def cross(a, b):
        return [a[1] * b[2] - a[2] * b[1], a[2] * b[0] - a[0] * b[2], a[0] * b[1] - a[1] * b[0]]

    def inner(a, b):
        return a[0] * b[0] + a[1] * b[1] + a[2] * b[2]

    def stacked(values, first, last):
        return jnp.concatenate([jnp.concatenate(values[n], axis=0) for n in range(first, last)], axis=1)

    messages = [[] for _ in range(chunks)]
    for step in range(steps):
        for h in range(halves):
            at, s, v, u, w = edge_inputs(step, h)
            q = inner(u, v)
            along = w[2] * s + w[5] * q
            keep = w[3] - w[5] * third_part
            turned = cross([w[4] * x for x in v], u)
            new = [w[0] * s + w[1] * q] + [along * u[a] + keep * v[a] + turned[a] for a in range(3)]
            for part, value in enumerate(new):
                messages[part * halves + h].append(value)
    centre = lax.broadcasted_iota(jnp.int32, (atoms, edges), 1) % atoms
    mine = (centre == lax.broadcasted_iota(jnp.int32, (atoms, edges), 0)).astype(f32).astype(bf16)
    summed = dot(mine, stacked(messages, 0, chunks), (1, 0))

    cotangents = []
    terms = []
    for h in range(halves):
        lanes = slice(h * LANES, (h + 1) * LANES)
        sums = [summed[:, (p * halves + h) * LANES : (p * halves + h + 1) * LANES] for p in range(4)]
        s_out = scalars[:, lanes] + scale * sums[0]
        v_out = [vectors[a, :, lanes] + scale * sums[1 + a] for a in range(3)]
        c = coeff[:, lanes]
        g = gains[:, lanes]
        sig = sigmoid(s_out)
        terms.append(c * s_out * sig + g * inner(v_out, v_out))
        cot_s = readout * c * sig * (1.0 + s_out * (1.0 - sig))
        cot_v = [(2.0 * readout) * g * v_out[a] for a in range(3)]
        cotangents.append([cot_s] + cot_v)
    total = sum(terms[1:], terms[0])
    energies[...] = readout * dot(jnp.ones((8, LANES), f32), total, (1, 1), HIGHEST)[0:1, :]

    dfar, dweights, dsteer = [[[] for _ in range(n * halves)] for n in (4, 6, 3)]
    pulled = [[(scale * jnp.concatenate([x, x], axis=0)).astype(bf16) for x in c] for c in cotangents]
    for step in range(steps):
        for h in range(halves):
            at, s, v, u, w = edge_inputs(step, h)
            cs, *cv = pulled[h]
            q = inner(u, v)
            along = w[2] * s + w[5] * q
            keep = w[3] - w[5] * third_part
            d = inner(cv, u)
            turn = cross(u, cv)
            spin = cross(cv, v)
            both = inner(cv, v)
            dq = cs * w[1] + w[5] * d
            ds = cs * w[0] + w[2] * d
            dv = [dq * u[a] + keep * cv[a] + w[4] * turn[a] for a in range(3)]
            du = [dq * v[a] + along * cv[a] + w[4] * spin[a] for a in range(3)]
            dw = [cs * s, cs * q, s * d, both, inner(u, spin), q * d - both * third_part]
            for part, value in enumerate([ds] + dv):
                dfar[part * halves + h].append(value)
            for n in range(6):
                dweights[n * halves + h].append(dw[n])
            for a in range(3):
                dsteer[a * halves + h].append(du[a])

    def put(chunk, value):
        for members, ref in zip(sinks, grads):
            for n, block in enumerate(members):
                piece = value[block * atoms : (block + 1) * atoms, :]
                at = n * packet + chunk * atoms
                if block == 0:
                    piece = piece + cotangents[chunk % halves][chunk // halves]
                    own_out[chunk * atoms : (chunk + 1) * atoms, :] = piece
                    piece = jnp.zeros_like(piece)
                ref[at : at + atoms, :] = piece

    for chunk in range(chunks):
        put(chunk, dot(picks, stacked(dfar, chunk, chunk + 1), (1, 0)))

    dhidden_two = dot(third[...], stacked(dweights, 0, 6 * halves), (1, 1))
    dpre_two = dhidden_two * usable[...] * sig_two * (1.0 + pre_two * (1.0 - sig_two))
    dhidden_one = dot(second[...], dpre_two.astype(bf16), (1, 0))
    dpre_one = dhidden_one * sig_one * (1.0 + pre_one * (1.0 - sig_one))
    dgauss = dot(first[...], dpre_one.astype(bf16), (1, 0))
    ddistance = jnp.sum(dgauss * gauss * off, axis=0, keepdims=True) * (-2.0 * SHARPNESS)
    gather = (
        lax.broadcasted_iota(jnp.int32, (8, 3 * channels), 1) // channels
        == lax.broadcasted_iota(jnp.int32, (8, 3 * channels), 0)
    ).astype(f32).astype(bf16)
    ddirection = dot(gather, stacked(dsteer, 0, 3 * halves), (1, 1))
    radial = jnp.sum(ddirection * direction, axis=0, keepdims=True)
    inv = 1.0 / distance
    dapart = ddirection * inv + (ddistance - radial * inv) * direction
    dspots = joined(dot(thirds(dapart), contrast, (1, 1)), 8)

    for members, ref in zip(sinks, grads):
        for n, block in enumerate(members):
            at = n * packet + chunks * atoms
            piece = dspots[:, block * atoms : (block + 1) * atoms]
            if block == 0:
                own_out[chunks * atoms :, :] = jnp.zeros((atoms, LANES), f32)
                own_out[chunks * atoms :, 0:atoms] = piece
                piece = jnp.zeros_like(piece)
            ref[at : at + atoms, :] = jnp.zeros((atoms, LANES), f32)
            ref[at : at + atoms, 0:atoms] = piece


def finish_kernel(energies_in, own, lands, *rest):
    parts = rest[:-8]
    energies, forces, grad_scalars, grad_vectors, moved, scalar_rows, vector_rows, sems = rest[-8:]
    atoms, channels = scalar_rows.shape
    halves = channels // LANES
    chunks = 4 * halves
    copies = [
        pltpu.make_async_copy(a, b, sems.at[n])
        for n, (a, b) in enumerate([
            (energies_in, energies), (moved, forces), (scalar_rows, grad_scalars), (vector_rows, grad_vectors),
        ])
    ]
    copies[0].start()
    value = parts[0][...]
    for ref in parts[1:]:
        value = value + ref[...]
    ghost = [value[c * atoms : (c + 1) * atoms, :] for c in range(chunks + 1)]
    land = lands[...].astype(jnp.bfloat16)
    sums = dot(land, thirds(jnp.concatenate(ghost[:chunks], axis=1)), (1, 0))
    for part in (1, 2, 3, 0):
        for h in range(halves):
            chunk = part * halves + h
            total = own[chunk * atoms : (chunk + 1) * atoms, :] + sums[:, chunk * LANES : (chunk + 1) * LANES]
            lanes = slice(h * LANES, (h + 1) * LANES)
            if part:
                vector_rows[part - 1, :, lanes] = total
            else:
                scalar_rows[:, lanes] = total
        if part == 3:
            copies[3].start()
    copies[2].start()
    spots = joined(dot(thirds(ghost[chunks][:, 0:atoms]), land[:, 0:atoms], (1, 1)), atoms)
    moved[...] = -(own[chunks * atoms :, 0:atoms] + spots)[0:3, :]
    copies[1].start()
    for copy in copies:
        copy.wait()


VMEM = pl.BlockSpec(memory_space=pltpu.VMEM)
SMEM = pl.BlockSpec(memory_space=pltpu.SMEM)


def shards(
    places, scalars, vectors, species, bound_rows, bound_count, neighbour_ids, neighbour_count,
    radial_first, radial_second, radial_third, energy_table, vector_gains,
):
    f32 = jnp.float32
    atoms, channels = scalars.shape
    places, vectors = places.T, vectors.transpose(1, 0, 2)
    boundary = bound_rows.shape[0]
    assert boundary == atoms == 8
    slots = neighbour_ids.shape[0]
    edges = slots * atoms
    halves = channels // LANES
    chunks = 4 * halves
    packet_rows = (chunks + 1) * boundary

    packet = pl.pallas_call(
        pack_kernel,
        out_shape=jax.ShapeDtypeStruct((packet_rows, LANES), f32),
        in_specs=[SMEM] + [pl.BlockSpec(memory_space=pltpu.HBM)] * 4,
        out_specs=VMEM,
        scratch_shapes=[
            pltpu.SMEM(bound_rows.shape, jnp.int32),
            pltpu.VMEM(places.shape, f32),
            pltpu.VMEM(scalars.shape, f32),
            pltpu.VMEM(vectors.shape, f32),
            pltpu.SemaphoreType.DMA((4,)),
        ],
        compiler_params=pltpu.CompilerParams(vmem_limit_bytes=2 << 20),
        name="pack",
    )(bound_count, *[pltpu.with_memory_space_constraint(x, pltpu.HBM) for x in (bound_rows, places, scalars, vectors)])

    perms = {axis: sides(lax.axis_size(axis)) for axis in AXES}
    wide = {axis: 1 + len(perms[axis]) for axis in AXES}
    per_plane = wide["gx"] * wide["gy"]
    rows = per_plane * wide["gz"] * atoms
    beside_x = [lax.ppermute(packet, "gx", pairs) for pairs in perms["gx"]]
    beside_y = [lax.ppermute(packet, "gy", pairs) for pairs in perms["gy"]]
    across = jnp.concatenate(beside_x, axis=0)
    across, ids, counts = lax.optimization_barrier((across, neighbour_ids.T, neighbour_count.reshape(1, atoms)))
    plain = [
        places, scalars, vectors, radial_first, radial_second, radial_third, vector_gains.reshape(1, channels),
    ]
    parities = jnp.stack([lax.axis_index(a) % 2 if lax.axis_size(a) % 2 == 0 else 0 for a in AXES])
    prepared = pl.pallas_call(
        functools.partial(prep_kernel, tuple(wide[a] for a in AXES)),
        out_shape=[
            jax.ShapeDtypeStruct((rows, edges), jnp.bfloat16),
            jax.ShapeDtypeStruct((rows, edges), jnp.bfloat16),
            jax.ShapeDtypeStruct((8, edges), f32),
            jax.ShapeDtypeStruct((1, edges), f32),
            jax.ShapeDtypeStruct((atoms, channels), f32),
            jax.ShapeDtypeStruct((atoms, 3 * atoms), f32),
        ]
        + [jax.ShapeDtypeStruct(x.shape, x.dtype) for x in plain],
        in_specs=[SMEM] + [VMEM] * (6 + len(plain)),
        out_specs=[VMEM] * (6 + len(plain)),
        compiler_params=pltpu.CompilerParams(vmem_limit_bytes=2 << 20),
        name="prep",
    )(
        parities, ids, counts, species.reshape(1, atoms), energy_table,
        bound_rows.reshape(1, boundary), bound_count.reshape(1, 1), *plain,
    )
    prepared, plain = prepared[:6], prepared[6:]
    *prepared, lands = prepared
    corners = [lax.ppermute(across, "gy", pairs) for pairs in perms["gy"]]
    cross = jnp.concatenate([packet, across] + beside_y, axis=0)
    tables = [packet, across] + beside_y + corners
    for pairs in perms["gz"]:
        tables.append(lax.ppermute(cross, "gz", pairs))
        tables += [lax.ppermute(c, "gz", pairs) for c in corners]
    blocks = tuple(t.shape[0] // packet_rows for t in tables)
    nx, ny = wide["gx"], wide["gy"]
    sinks = []
    for z in range(wide["gz"]):
        first = z * per_plane
        sinks.append(tuple(range(first, first + nx)))
        for y in range(1, ny):
            corner = first + nx + ny - 1 + (y - 1) * (nx - 1)
            sinks.append((first + nx + y - 1, *range(corner, corner + nx - 1)))

    geometry = (atoms, slots, channels, blocks, tuple(sinks))
    out = pl.pallas_call(
        functools.partial(core_kernel, geometry),
        out_shape=[
            jax.ShapeDtypeStruct((1, atoms), f32),
            jax.ShapeDtypeStruct(((chunks + 1) * atoms, LANES), f32),
        ]
        + [jax.ShapeDtypeStruct((len(n) * packet_rows, LANES), f32) for n in sinks],
        in_specs=[VMEM] * (12 + len(tables)),
        out_specs=[VMEM] * (2 + len(sinks)),
        scratch_shapes=[
            pltpu.VMEM((rows, chunks * LANES), jnp.bfloat16),
            pltpu.VMEM((edges, 6 * channels), f32),
            pltpu.VMEM((edges, chunks * LANES), f32),
            pltpu.VMEM((edges, 3 * LANES), f32),
            pltpu.VMEM((atoms, rows), f32),
        ],
        compiler_params=pltpu.CompilerParams(vmem_limit_bytes=16 << 20),
        name="edges",
    )(
        *prepared, *plain, *tables,
    )
    energies, own, *grads = out

    lines = grads[:ny]
    for n, pairs in enumerate(perms["gz"]):
        back = [lax.ppermute(grads[(n + 1) * ny + y], "gz", inverse(pairs)) for y in range(ny)]
        lines = [a + b for a, b in zip(lines, back)]
    line = lines[0]
    for n, pairs in enumerate(perms["gy"]):
        line = line + lax.ppermute(lines[n + 1], "gy", inverse(pairs))
    parts = [line[:packet_rows]]
    for n, pairs in backwards(perms["gx"]):
        parts.append(lax.ppermute(line[(n + 1) * packet_rows : (n + 2) * packet_rows], "gx", inverse(pairs)))

    energies, forces, grad_scalars, grad_vectors = pl.pallas_call(
        finish_kernel,
        out_shape=[
            jax.ShapeDtypeStruct((1, atoms), f32),
            jax.ShapeDtypeStruct((3, atoms), f32),
            jax.ShapeDtypeStruct((atoms, channels), f32),
            jax.ShapeDtypeStruct((3, atoms, channels), f32),
        ],
        in_specs=[VMEM] * (3 + len(parts)),
        out_specs=[pl.BlockSpec(memory_space=pltpu.HBM)] * 4,
        scratch_shapes=[
            pltpu.VMEM((3, atoms), f32),
            pltpu.VMEM((atoms, channels), f32),
            pltpu.VMEM((3, atoms, channels), f32),
            pltpu.SemaphoreType.DMA((4,)),
        ],
        compiler_params=pltpu.CompilerParams(vmem_limit_bytes=2 << 20),
        name="finish",
    )(energies, own, lands, *parts)
    return energies.reshape(atoms), forces.T, grad_scalars, grad_vectors.transpose(1, 0, 2)


def solution(mesh):
    every = AXES
    in_specs = (
        P(every, None), P(every, None), P(every, None, None), P(every), P(every), P(every),
        P(None, every), P(every), P(), P(), P(), P(), P(),
    )
    out_specs = (P(every), P(every, None), P(every, None), P(every, None, None))

    return jax.shard_map(shards, mesh=mesh, in_specs=in_specs, out_specs=out_specs, check_vma=False)
```

```python
import functools

import jax
import jax.numpy as jnp
from jax import lax
from jax.experimental import pallas as pl
from jax.experimental.pallas import tpu as pltpu
from jax.sharding import PartitionSpec as P


SOFTENING = 0.25
SHARPNESS = 2.0
FIRST_CENTRE = 0.5
SPACING = 0.4
EDGE = 1.0
LANES = 128
HIGHEST = lax.Precision.HIGHEST
AXES = ("gx", "gy", "gz")


def dot(a, b, dims, precision=None):
    return lax.dot_general(
        a, b, ((dims[:1], dims[1:]), ((), ())), precision=precision,
        preferred_element_type=jnp.float32,
    )


def thirds(x, axis=0):
    high = x.astype(jnp.bfloat16).astype(jnp.float32)
    rest = x - high
    middle = rest.astype(jnp.bfloat16).astype(jnp.float32)
    return jnp.concatenate([high, middle, rest - middle], axis=axis).astype(jnp.bfloat16)


def joined(x, rows):
    return x[0:rows, :] + (x[rows : 2 * rows, :] + x[2 * rows :, :])


def sides(size):
    if size == 1:
        return []
    if size == 2:
        return [[(0, 1), (1, 0)]]
    if size % 2:
        return [[((i + 1) % size, i) for i in range(size)], [(i, (i + 1) % size) for i in range(size)]]
    pairs = [[(i, (i + 1) % size) for i in range(first, size, 2)] for first in (0, 1)]
    return [half + [(b, a) for a, b in half] for half in pairs]


def inverse(pairs):
    return [(b, a) for a, b in pairs]


def pack_kernel(
    bound_count, bound_rows_in, places_in, scalars_in, vectors_in, out,
    bound_rows, places, scalars, vectors, sems,
):
    pairs = [(bound_rows_in, bound_rows), (places_in, places), (scalars_in, scalars), (vectors_in, vectors)]
    copies = [pltpu.make_async_copy(a, b, sems.at[n]) for n, (a, b) in enumerate(pairs)]
    for copy in copies:
        copy.start()
    for copy in copies:
        copy.wait()
    boundary = bound_rows.shape[0]
    channels = scalars.shape[1]
    halves = channels // LANES
    source = lax.broadcasted_iota(jnp.int32, (places.shape[1], LANES), 0)
    lane = lax.broadcasted_iota(jnp.int32, (places.shape[1], LANES), 1)
    moved = jnp.zeros(source.shape, jnp.float32)
    for slot in range(boundary):
        atom = bound_rows[slot]
        alive = jnp.where(slot < bound_count[0], 1.0, 0.0).astype(jnp.float32)
        rows = [scalars[pl.ds(atom, 1), :]] + [vectors[a, pl.ds(atom, 1), :] for a in range(3)]
        for part, row in enumerate(rows):
            row = row * alive
            for h in range(halves):
                at = (part * halves + h) * boundary + slot
                out[at : at + 1, :] = row[:, h * LANES : (h + 1) * LANES]
        moved = jnp.where((lane == slot) & (source == atom), alive, moved)
    spots = dot(places[...], moved, (1, 0), HIGHEST)
    out[4 * halves * boundary :, :] = jnp.concatenate([spots, jnp.zeros((boundary - 3, LANES), jnp.float32)], axis=0)


def prep_kernel(
    wide, parities, ids, counts, species, energy_table, bound_rows, bound_count, *rest
):
    atoms, slots = ids.shape
    edges = atoms * slots
    f32 = jnp.float32
    count = (len(rest) - 6) // 2
    passed, (picks, contrast, displace, usable, coeff, lands), copied = rest[:count], rest[count:-count], rest[-count:]
    for a, b in zip(passed, copied):
        b[...] = a[...]
    lane = lax.broadcasted_iota(jnp.int32, (atoms, edges), 1)
    mine = lane % atoms == lax.broadcasted_iota(jnp.int32, (atoms, edges), 0)
    slot_lane = lax.broadcasted_iota(jnp.int32, (slots, edges), 1) // atoms
    belongs = (slot_lane == lax.broadcasted_iota(jnp.int32, (slots, edges), 0)).astype(f32)
    spread = dot(ids[...].astype(f32), belongs, (1, 0), HIGHEST)
    where = jnp.sum(jnp.where(mine, spread, 0.0), axis=0, keepdims=True).astype(jnp.int32)
    live = dot(jnp.broadcast_to(counts[...], (8, atoms)).astype(f32), mine.astype(f32), (1, 0), HIGHEST)[0:1, :]
    usable[...] = (slot_lane[0:1, :].astype(f32) < live).astype(f32)
    owned = where < atoms
    ghost = jnp.maximum(where - atoms, 0)
    block = ghost // atoms
    offsets = [block // 9 - 1, (block // 3) % 3 - 1, block % 3 - 1]
    at = []
    for axis, offset in enumerate(offsets):
        if wide[axis] == 1:
            at.append(jnp.zeros_like(offset))
        elif wide[axis] == 2:
            at.append(jnp.abs(offset))
        else:
            at.append(jnp.where(offset == 0, 0, jnp.where(offset == 1 - 2 * parities[axis], 1, 2)))
    inside = jnp.where(
        at[1] == 0, at[0],
        jnp.where(at[0] == 0, wide[0] - 1 + at[1], wide[0] + wide[1] - 1 + (at[1] - 1) * (wide[0] - 1) + at[0] - 1),
    )
    stored = at[2] * (wide[0] * wide[1]) + inside
    row_of = jnp.where(owned, where, stored * atoms + ghost % atoms)
    row_index = lax.broadcasted_iota(jnp.int32, contrast.shape, 0)
    centre = lax.broadcasted_iota(jnp.int32, contrast.shape, 1) % atoms
    chosen = (row_index == row_of).astype(f32)
    picks[...] = chosen.astype(jnp.bfloat16)
    contrast[...] = (chosen - (row_index == centre).astype(f32)).astype(jnp.bfloat16)
    kinds = (lax.broadcasted_iota(jnp.int32, (energy_table.shape[0], atoms), 0) == species[...]).astype(f32)
    coeff[...] = dot(kinds, energy_table[...], (0, 0), HIGHEST)
    slot = lax.broadcasted_iota(jnp.int32, (atoms, atoms), 1)
    target = lax.broadcasted_iota(jnp.int32, (atoms, atoms), 0)
    land = ((target == bound_rows[...]) & (slot < bound_count[...])).astype(f32)
    lands[...] = jnp.concatenate([land, land, land], axis=1)
    shift = [jnp.where(owned, 0, offset).astype(f32) * EDGE for offset in offsets]
    displace[...] = jnp.concatenate(shift + [jnp.zeros((5, edges), f32)], axis=0)


def sigmoid(x):
    return 1.0 / (1.0 + jnp.exp(-x))


def core_kernel(
    geometry,
    picks_in, contrast_in, displace, usable, coeff, places, scalars, vectors, first, second, third,
    gains, *rest,
):
    atoms, slots, channels, blocks, sinks = geometry
    tables = len(blocks)
    ghosts = rest[:tables]
    energies, own_out = rest[tables : tables + 2]
    grads = rest[tables + 2 : tables + 2 + len(sinks)]
    table, weights, far, steer, place_rows = rest[tables + 2 + len(sinks) :]
    halves = channels // LANES
    chunks = 4 * halves
    edges = atoms * slots
    packet = (chunks + 1) * atoms
    scale = slots ** (-0.5)
    readout = channels ** (-0.25)
    f32, bf16 = jnp.float32, jnp.bfloat16

    def pieces(chunk, own):
        parts = []
        for which, ref in enumerate(ghosts):
            for block in range(blocks[which]):
                if which == 0 and block == 0:
                    parts.append(own)
                else:
                    at = block * packet + chunk * atoms
                    parts.append(ref[at : at + atoms, :])
        return jnp.concatenate(parts, axis=0)

    picks, contrast = picks_in[...], contrast_in[...]

    row = 0
    for which, ref in enumerate(ghosts):
        for block in range(blocks[which]):
            at = block * packet + chunks * atoms
            if row:
                place_rows[:, row : row + atoms] = ref[at : at + atoms, 0:atoms]
            else:
                place_rows[0:3, 0:atoms] = places[...]
                place_rows[3:, 0:atoms] = jnp.zeros((atoms - 3, atoms), f32)
            row += atoms
    apart = joined(dot(thirds(place_rows[...]), contrast, (1, 0)), 8) + displace[...]
    distance = jnp.sqrt(jnp.sum(apart * apart, axis=0, keepdims=True) + SOFTENING)
    direction = apart / distance
    centres = FIRST_CENTRE + SPACING * lax.broadcasted_iota(jnp.int32, (first.shape[0], edges), 0).astype(f32)
    off = distance - centres
    gauss = jnp.exp(-SHARPNESS * off * off)
    basis = jnp.concatenate([gauss, gauss * off * (-2.0 * SHARPNESS)], axis=1)
    hidden = dot(first[...], basis.astype(bf16), (0, 0))
    for layer in (second[...], None):
        value, slope = hidden[:, 0:edges], hidden[:, edges:]
        sig = sigmoid(value)
        value, slope = value * sig, slope * sig * (1.0 + value * (1.0 - sig))
        if layer is None:
            value, slope = value * usable[...], slope * usable[...]
        hidden = jnp.concatenate([value, slope], axis=1).astype(bf16)
        if layer is not None:
            hidden = dot(layer, hidden, (0, 0))
    weights[0:edges, :] = dot(hidden[:, 0:edges], third[...], (0, 0))
    spread = (
        lax.broadcasted_iota(jnp.int32, (8, 3 * LANES), 1) // LANES
        == lax.broadcasted_iota(jnp.int32, (8, 3 * LANES), 0)
    ).astype(f32).astype(bf16)
    steer[...] = dot(direction.astype(bf16), spread, (0, 0))

    for part in range(4):
        for h in range(halves):
            chunk = part * halves + h
            lanes = slice(h * LANES, (h + 1) * LANES)
            own = scalars[:, lanes] if part == 0 else vectors[part - 1, :, lanes]
            table[:, chunk * LANES : (chunk + 1) * LANES] = pieces(chunk, own).astype(bf16)
    far[...] = dot(picks, table[...], (0, 0))

    tile = 2 * atoms
    steps = edges // tile
    third_part = jnp.asarray(1.0 / 3.0, bf16)

    def edge_inputs(step, h):
        at = slice(step * tile, (step + 1) * tile)
        s = far[at, h * LANES : (h + 1) * LANES].astype(bf16)
        v = [far[at, ((1 + a) * halves + h) * LANES : ((1 + a) * halves + h + 1) * LANES].astype(bf16) for a in range(3)]
        u = [steer[at, a * LANES : (a + 1) * LANES].astype(bf16) for a in range(3)]
        w = [weights[at, n * channels + h * LANES : n * channels + (h + 1) * LANES].astype(bf16) for n in range(6)]
        return at, s, v, u, w

    def slopes(step, h):
        at = slice(edges + step * tile, edges + (step + 1) * tile)
        return [weights[at, n * channels + h * LANES : n * channels + (h + 1) * LANES].astype(bf16) for n in range(6)]

    def cross(a, b):
        return [a[1] * b[2] - a[2] * b[1], a[2] * b[0] - a[0] * b[2], a[0] * b[1] - a[1] * b[0]]

    def inner(a, b):
        return a[0] * b[0] + a[1] * b[1] + a[2] * b[2]

    def stacked(values, first, last):
        return jnp.concatenate([jnp.concatenate(values[n], axis=0) for n in range(first, last)], axis=1)

    messages = [[] for _ in range(chunks)]
    for step in range(steps):
        for h in range(halves):
            at, s, v, u, w = edge_inputs(step, h)
            q = inner(u, v)
            along = w[2] * s + w[5] * q
            keep = w[3] - w[5] * third_part
            turned = cross([w[4] * x for x in v], u)
            new = [w[0] * s + w[1] * q] + [along * u[a] + keep * v[a] + turned[a] for a in range(3)]
            for part, value in enumerate(new):
                messages[part * halves + h].append(value)
    weights[edges:, :] = dot(hidden[:, edges:], third[...], (0, 0))
    centre = lax.broadcasted_iota(jnp.int32, (atoms, edges), 1) % atoms
    mine = (centre == lax.broadcasted_iota(jnp.int32, (atoms, edges), 0)).astype(f32).astype(bf16)
    summed = dot(mine, stacked(messages, 0, chunks), (1, 0))

    cotangents = []
    terms = []
    for h in range(halves):
        lanes = slice(h * LANES, (h + 1) * LANES)
        sums = [summed[:, (p * halves + h) * LANES : (p * halves + h + 1) * LANES] for p in range(4)]
        s_out = scalars[:, lanes] + scale * sums[0]
        v_out = [vectors[a, :, lanes] + scale * sums[1 + a] for a in range(3)]
        c = coeff[:, lanes]
        g = gains[:, lanes]
        sig = sigmoid(s_out)
        terms.append(c * s_out * sig + g * inner(v_out, v_out))
        cot_s = readout * c * sig * (1.0 + s_out * (1.0 - sig))
        cot_v = [(2.0 * readout) * g * v_out[a] for a in range(3)]
        cotangents.append([cot_s] + cot_v)
    total = sum(terms[1:], terms[0])
    energies[...] = readout * dot(jnp.ones((8, LANES), f32), total, (1, 1), HIGHEST)[0:1, :]

    dfar, dsteer = [[[] for _ in range(n * halves)] for n in (4, 5)]
    pulled = [[(scale * jnp.concatenate([x, x], axis=0)).astype(bf16) for x in c] for c in cotangents]
    for step in range(steps):
        for h in range(halves):
            at, s, v, u, w = edge_inputs(step, h)
            cs, *cv = pulled[h]
            q = inner(u, v)
            along = w[2] * s + w[5] * q
            keep = w[3] - w[5] * third_part
            d = inner(cv, u)
            turn = cross(u, cv)
            spin = cross(cv, v)
            dq = cs * w[1] + w[5] * d
            ds = cs * w[0] + w[2] * d
            dv = [dq * u[a] + keep * cv[a] + w[4] * turn[a] for a in range(3)]
            du = [dq * v[a] + along * cv[a] + w[4] * spin[a] for a in range(3)]
            g = slopes(step, h)
            stretch = [
                s * (cs * g[0] + d * g[2]) + q * (cs * g[1] + d * g[5]),
                inner(cv, v) * (g[3] - g[5] * third_part) + inner(u, spin) * g[4],
            ]
            for part, value in enumerate([ds] + dv):
                dfar[part * halves + h].append(value)
            for a, value in enumerate(du + stretch):
                dsteer[a * halves + h].append(value)

    def put(chunk, value):
        for members, ref in zip(sinks, grads):
            for n, block in enumerate(members):
                piece = value[block * atoms : (block + 1) * atoms, :]
                at = (n * chunks + chunk) * atoms
                if block == 0:
                    piece = piece + cotangents[chunk % halves][chunk // halves]
                    own_out[chunk * atoms : (chunk + 1) * atoms, :] = piece
                    piece = jnp.zeros_like(piece)
                ref[at : at + atoms, :] = piece

    for chunk in range(chunks):
        put(chunk, dot(picks, stacked(dfar, chunk, chunk + 1), (1, 0)))

    gather = (
        jnp.minimum(lax.broadcasted_iota(jnp.int32, (8, 5 * channels), 1) // channels, 3)
        == lax.broadcasted_iota(jnp.int32, (8, 5 * channels), 0)
    ).astype(f32).astype(bf16)
    ddirection = dot(gather, stacked(dsteer, 0, 5 * halves), (1, 1))
    ddistance = ddirection[3:4, :]
    radial = jnp.sum(ddirection * direction, axis=0, keepdims=True)
    inv = 1.0 / distance
    component = lax.broadcasted_iota(jnp.int32, (8, edges), 0) < 3
    dapart = jnp.where(component, ddirection * inv, 0.0) + (ddistance - radial * inv) * direction
    dspots = joined(dot(thirds(dapart), contrast, (1, 1)), 8)

    for members, ref in zip(sinks, grads):
        at = len(members) * chunks * atoms
        ref[at:, :] = jnp.zeros((atoms, LANES), f32)
        for n, block in enumerate(members):
            piece = dspots[:, block * atoms : (block + 1) * atoms]
            if block == 0:
                own_out[chunks * atoms :, :] = jnp.zeros((atoms, LANES), f32)
                own_out[chunks * atoms :, 0:atoms] = piece
            else:
                ref[at:, n * atoms : (n + 1) * atoms] = piece


def finish_kernel(energies_in, own, lands, *rest):
    parts = rest[:-8]
    energies, forces, grad_scalars, grad_vectors, moved, scalar_rows, vector_rows, sems = rest[-8:]
    atoms, channels = scalar_rows.shape
    halves = channels // LANES
    chunks = 4 * halves
    copies = [
        pltpu.make_async_copy(a, b, sems.at[n])
        for n, (a, b) in enumerate([
            (energies_in, energies), (moved, forces), (scalar_rows, grad_scalars), (vector_rows, grad_vectors),
        ])
    ]
    copies[0].start()
    values = [ref[0 : chunks * atoms, :] for ref in parts]
    value = sum(values[1:], values[0])
    spots = [ref[ref.shape[0] - atoms :, n * atoms : (n + 1) * atoms] for n, ref in enumerate(parts)]
    spots = sum(spots[1:], spots[0])
    ghost = [value[c * atoms : (c + 1) * atoms, :] for c in range(chunks)]
    land = lands[...].astype(jnp.bfloat16)
    sums = dot(land, thirds(jnp.concatenate(ghost, axis=1)), (1, 0))
    for part in (1, 2, 3, 0):
        for h in range(halves):
            chunk = part * halves + h
            total = own[chunk * atoms : (chunk + 1) * atoms, :] + sums[:, chunk * LANES : (chunk + 1) * LANES]
            lanes = slice(h * LANES, (h + 1) * LANES)
            if part:
                vector_rows[part - 1, :, lanes] = total
            else:
                scalar_rows[:, lanes] = total
        if part == 3:
            copies[3].start()
    copies[2].start()
    spots = joined(dot(thirds(spots), land[:, 0:atoms], (1, 1)), atoms)
    moved[...] = -(own[chunks * atoms :, 0:atoms] + spots)[0:3, :]
    copies[1].start()
    for copy in copies:
        copy.wait()


VMEM = pl.BlockSpec(memory_space=pltpu.VMEM)
SMEM = pl.BlockSpec(memory_space=pltpu.SMEM)


def shards(
    places, scalars, vectors, species, bound_rows, bound_count, neighbour_ids, neighbour_count,
    radial_first, radial_second, radial_third, energy_table, vector_gains,
):
    f32 = jnp.float32
    atoms, channels = scalars.shape
    places, vectors = places.T, vectors.transpose(1, 0, 2)
    boundary = bound_rows.shape[0]
    assert boundary == atoms == 8
    slots = neighbour_ids.shape[0]
    edges = slots * atoms
    halves = channels // LANES
    chunks = 4 * halves
    packet_rows = (chunks + 1) * boundary

    packet = pl.pallas_call(
        pack_kernel,
        out_shape=jax.ShapeDtypeStruct((packet_rows, LANES), f32),
        in_specs=[SMEM] + [pl.BlockSpec(memory_space=pltpu.HBM)] * 4,
        out_specs=VMEM,
        scratch_shapes=[
            pltpu.SMEM(bound_rows.shape, jnp.int32),
            pltpu.VMEM(places.shape, f32),
            pltpu.VMEM(scalars.shape, f32),
            pltpu.VMEM(vectors.shape, f32),
            pltpu.SemaphoreType.DMA((4,)),
        ],
        compiler_params=pltpu.CompilerParams(vmem_limit_bytes=2 << 20),
        name="pack",
    )(bound_count, *[pltpu.with_memory_space_constraint(x, pltpu.HBM) for x in (bound_rows, places, scalars, vectors)])

    perms = {axis: sides(lax.axis_size(axis)) for axis in AXES}
    wide = {axis: 1 + len(perms[axis]) for axis in AXES}
    per_plane = wide["gx"] * wide["gy"]
    rows = per_plane * wide["gz"] * atoms
    beside_x = [lax.ppermute(packet, "gx", pairs) for pairs in perms["gx"]]
    beside_y = [lax.ppermute(packet, "gy", pairs) for pairs in perms["gy"]]
    across = jnp.concatenate(beside_x, axis=0)
    across, ids, counts = lax.optimization_barrier((across, neighbour_ids.T, neighbour_count.reshape(1, atoms)))
    plain = [
        places, scalars, vectors, radial_first, radial_second, radial_third, vector_gains.reshape(1, channels),
    ]
    parities = jnp.stack([lax.axis_index(a) % 2 if lax.axis_size(a) % 2 == 0 else 0 for a in AXES])
    prepared = pl.pallas_call(
        functools.partial(prep_kernel, tuple(wide[a] for a in AXES)),
        out_shape=[
            jax.ShapeDtypeStruct((rows, edges), jnp.bfloat16),
            jax.ShapeDtypeStruct((rows, edges), jnp.bfloat16),
            jax.ShapeDtypeStruct((8, edges), f32),
            jax.ShapeDtypeStruct((1, edges), f32),
            jax.ShapeDtypeStruct((atoms, channels), f32),
            jax.ShapeDtypeStruct((atoms, 3 * atoms), f32),
        ]
        + [jax.ShapeDtypeStruct(x.shape, x.dtype) for x in plain],
        in_specs=[SMEM] + [VMEM] * (6 + len(plain)),
        out_specs=[VMEM] * (6 + len(plain)),
        compiler_params=pltpu.CompilerParams(vmem_limit_bytes=2 << 20),
        name="prep",
    )(
        parities, ids, counts, species.reshape(1, atoms), energy_table,
        bound_rows.reshape(1, boundary), bound_count.reshape(1, 1), *plain,
    )
    prepared, plain = prepared[:6], prepared[6:]
    *prepared, lands = prepared
    corners = [lax.ppermute(across, "gy", pairs) for pairs in perms["gy"]]
    cross = jnp.concatenate([packet, across] + beside_y, axis=0)
    tables = [packet, across] + beside_y + corners
    for pairs in perms["gz"]:
        tables.append(lax.ppermute(cross, "gz", pairs))
        tables += [lax.ppermute(c, "gz", pairs) for c in corners]
    blocks = tuple(t.shape[0] // packet_rows for t in tables)
    nx, ny = wide["gx"], wide["gy"]
    sinks = []
    for z in range(wide["gz"]):
        first = z * per_plane
        sinks.append(tuple(range(first, first + nx)))
        for y in range(1, ny):
            corner = first + nx + ny - 1 + (y - 1) * (nx - 1)
            sinks.append((first + nx + y - 1, *range(corner, corner + nx - 1)))

    geometry = (atoms, slots, channels, blocks, tuple(sinks))
    out = pl.pallas_call(
        functools.partial(core_kernel, geometry),
        out_shape=[
            jax.ShapeDtypeStruct((1, atoms), f32),
            jax.ShapeDtypeStruct(((chunks + 1) * atoms, LANES), f32),
        ]
        + [jax.ShapeDtypeStruct(((len(n) * chunks + 1) * boundary, LANES), f32) for n in sinks],
        in_specs=[VMEM] * (12 + len(tables)),
        out_specs=[VMEM] * (2 + len(sinks)),
        scratch_shapes=[
            pltpu.VMEM((rows, chunks * LANES), jnp.bfloat16),
            pltpu.VMEM((2 * edges, 6 * channels), f32),
            pltpu.VMEM((edges, chunks * LANES), f32),
            pltpu.VMEM((edges, 3 * LANES), f32),
            pltpu.VMEM((atoms, rows), f32),
        ],
        compiler_params=pltpu.CompilerParams(vmem_limit_bytes=16 << 20),
        name="edges",
    )(
        *prepared, *plain, *tables,
    )
    energies, own, *grads = out

    lines = grads[:ny]
    for n, pairs in enumerate(perms["gz"]):
        back = [lax.ppermute(grads[(n + 1) * ny + y], "gz", inverse(pairs)) for y in range(ny)]
        lines = [a + b for a, b in zip(lines, back)]
    line = lines[0]
    for n, pairs in enumerate(perms["gy"]):
        line = line + lax.ppermute(lines[n + 1], "gy", inverse(pairs))
    parts, span = [line], chunks * boundary
    for n, pairs in enumerate(perms["gx"]):
        value = jnp.concatenate([line[(n + 1) * span : (n + 2) * span], line[-boundary:]], axis=0)
        parts.append(lax.ppermute(value, "gx", inverse(pairs)))

    energies, forces, grad_scalars, grad_vectors = pl.pallas_call(
        finish_kernel,
        out_shape=[
            jax.ShapeDtypeStruct((1, atoms), f32),
            jax.ShapeDtypeStruct((3, atoms), f32),
            jax.ShapeDtypeStruct((atoms, channels), f32),
            jax.ShapeDtypeStruct((3, atoms, channels), f32),
        ],
        in_specs=[VMEM] * (3 + len(parts)),
        out_specs=[pl.BlockSpec(memory_space=pltpu.HBM)] * 4,
        scratch_shapes=[
            pltpu.VMEM((3, atoms), f32),
            pltpu.VMEM((atoms, channels), f32),
            pltpu.VMEM((3, atoms, channels), f32),
            pltpu.SemaphoreType.DMA((4,)),
        ],
        compiler_params=pltpu.CompilerParams(vmem_limit_bytes=2 << 20),
        name="finish",
    )(energies, own, lands, *parts)
    return energies.reshape(atoms), forces.T, grad_scalars, grad_vectors.transpose(1, 0, 2)


def solution(mesh):
    every = AXES
    in_specs = (
        P(every, None), P(every, None), P(every, None, None), P(every), P(every), P(every),
        P(None, every), P(every), P(), P(), P(), P(), P(),
    )
    out_specs = (P(every), P(every, None), P(every, None), P(every, None, None))

    return jax.shard_map(shards, mesh=mesh, in_specs=in_specs, out_specs=out_specs, check_vma=False)
```

```python
import functools

import jax
import jax.numpy as jnp
from jax import lax
from jax.experimental import pallas as pl
from jax.experimental.pallas import tpu as pltpu
from jax.sharding import PartitionSpec as P


SOFTENING = 0.25
SHARPNESS = 2.0
FIRST_CENTRE = 0.5
SPACING = 0.4
EDGE = 1.0
LANES = 128
HIGHEST = lax.Precision.HIGHEST
AXES = ("gx", "gy", "gz")


def dot(a, b, dims, precision=None):
    return lax.dot_general(
        a, b, ((dims[:1], dims[1:]), ((), ())), precision=precision,
        preferred_element_type=jnp.float32,
    )


def thirds(x, axis=0):
    high = x.astype(jnp.bfloat16).astype(jnp.float32)
    rest = x - high
    middle = rest.astype(jnp.bfloat16).astype(jnp.float32)
    return jnp.concatenate([high, middle, rest - middle], axis=axis).astype(jnp.bfloat16)


def joined(x, rows):
    return x[0:rows, :] + (x[rows : 2 * rows, :] + x[2 * rows :, :])


def sides(size):
    if size == 1:
        return []
    if size == 2:
        return [[(0, 1), (1, 0)]]
    if size % 2:
        return [[((i + 1) % size, i) for i in range(size)], [(i, (i + 1) % size) for i in range(size)]]
    pairs = [[(i, (i + 1) % size) for i in range(first, size, 2)] for first in (0, 1)]
    return [half + [(b, a) for a, b in half] for half in pairs]


def inverse(pairs):
    return [(b, a) for a, b in pairs]


def pack_kernel(
    bound_count, bound_rows_in, places_in, scalars_in, vectors_in, out,
    bound_rows, places, scalars, vectors, sems,
):
    pairs = [(bound_rows_in, bound_rows), (places_in, places), (scalars_in, scalars), (vectors_in, vectors)]
    copies = [pltpu.make_async_copy(a, b, sems.at[n]) for n, (a, b) in enumerate(pairs)]
    for copy in copies:
        copy.start()
    boundary = bound_rows.shape[0]
    halves = scalars.shape[1] // LANES
    source = lax.broadcasted_iota(jnp.int32, (places.shape[1], LANES), 0)
    lane = lax.broadcasted_iota(jnp.int32, (places.shape[1], LANES), 1)
    moved = jnp.zeros(source.shape, jnp.float32)
    copies[0].wait()
    atoms = [bound_rows[slot] for slot in range(boundary)]
    alive = [jnp.where(slot < bound_count[0], 1.0, 0.0).astype(jnp.float32) for slot in range(boundary)]
    for slot in range(boundary):
        moved = jnp.where((lane == slot) & (source == atoms[slot]), alive[slot], moved)
    copies[1].wait()
    spots = joined(dot(thirds(jnp.concatenate([places[...], jnp.zeros((5, source.shape[0]), jnp.float32)], axis=0)),
                       moved.astype(jnp.bfloat16), (1, 0)), 8)
    copies[2].wait()
    copies[3].wait()
    for slot in range(boundary):
        rows = [scalars[pl.ds(atoms[slot], 1), :]] + [vectors[a, pl.ds(atoms[slot], 1), :] for a in range(3)]
        for part, row in enumerate(rows):
            row = row * alive[slot]
            for h in range(halves):
                at = (part * halves + h) * boundary + slot
                out[at : at + 1, :] = row[:, h * LANES : (h + 1) * LANES]
    out[4 * halves * boundary :, :] = spots


def prep_kernel(
    wide, parities, ids, counts, species, energy_table, bound_rows, bound_count, *rest
):
    atoms, slots = ids.shape
    edges = atoms * slots
    f32 = jnp.float32
    count = (len(rest) - 6) // 2
    passed, (picks, contrast, displace, usable, coeff, lands), copied = rest[:count], rest[count:-count], rest[-count:]
    for a, b in zip(passed, copied):
        b[...] = a[...]
    lane = lax.broadcasted_iota(jnp.int32, (atoms, edges), 1)
    mine = lane % atoms == lax.broadcasted_iota(jnp.int32, (atoms, edges), 0)
    slot_lane = lax.broadcasted_iota(jnp.int32, (slots, edges), 1) // atoms
    belongs = (slot_lane == lax.broadcasted_iota(jnp.int32, (slots, edges), 0)).astype(f32)
    spread = dot(ids[...].astype(f32), belongs, (1, 0), HIGHEST)
    where = jnp.sum(jnp.where(mine, spread, 0.0), axis=0, keepdims=True).astype(jnp.int32)
    live = dot(jnp.broadcast_to(counts[...], (8, atoms)).astype(f32), mine.astype(f32), (1, 0), HIGHEST)[0:1, :]
    usable[...] = (slot_lane[0:1, :].astype(f32) < live).astype(f32)
    owned = where < atoms
    ghost = jnp.maximum(where - atoms, 0)
    block = ghost // atoms
    offsets = [block // 9 - 1, (block // 3) % 3 - 1, block % 3 - 1]
    at = []
    for axis, offset in enumerate(offsets):
        if wide[axis] == 1:
            at.append(jnp.zeros_like(offset))
        elif wide[axis] == 2:
            at.append(jnp.abs(offset))
        else:
            at.append(jnp.where(offset == 0, 0, jnp.where(offset == 1 - 2 * parities[axis], 1, 2)))
    inside = jnp.where(
        at[1] == 0, at[0],
        jnp.where(at[0] == 0, wide[0] - 1 + at[1], wide[0] + wide[1] - 1 + (at[1] - 1) * (wide[0] - 1) + at[0] - 1),
    )
    stored = at[2] * (wide[0] * wide[1]) + inside
    row_of = jnp.where(owned, where, stored * atoms + ghost % atoms)
    row_index = lax.broadcasted_iota(jnp.int32, contrast.shape, 0)
    centre = lax.broadcasted_iota(jnp.int32, contrast.shape, 1) % atoms
    chosen = (row_index == row_of).astype(f32)
    picks[...] = chosen.astype(jnp.bfloat16)
    contrast[...] = (chosen - (row_index == centre).astype(f32)).astype(jnp.bfloat16)
    kinds = (lax.broadcasted_iota(jnp.int32, (energy_table.shape[0], atoms), 0) == species[...]).astype(f32)
    coeff[...] = dot(kinds, energy_table[...], (0, 0), HIGHEST)
    slot = lax.broadcasted_iota(jnp.int32, (atoms, atoms), 1)
    target = lax.broadcasted_iota(jnp.int32, (atoms, atoms), 0)
    land = ((target == bound_rows[...]) & (slot < bound_count[...])).astype(f32)
    lands[...] = jnp.concatenate([land, land, land], axis=1)
    shift = [jnp.where(owned, 0, offset).astype(f32) * EDGE for offset in offsets]
    displace[...] = jnp.concatenate(shift + [jnp.zeros((5, edges), f32)], axis=0)


def sigmoid(x):
    return 1.0 / (1.0 + jnp.exp(-x))


def core_kernel(
    geometry,
    picks_in, contrast_in, displace, usable, coeff, places, scalars, vectors, first, second, third,
    gains, *rest,
):
    atoms, slots, channels, blocks, sinks = geometry
    tables = len(blocks)
    ghosts = rest[:tables]
    energies, own_out = rest[tables : tables + 2]
    grads = rest[tables + 2 : tables + 2 + len(sinks)]
    weights, far, steer, place_rows = rest[tables + 2 + len(sinks) :]
    halves = channels // LANES
    chunks = 4 * halves
    edges = atoms * slots
    packet = (chunks + 1) * atoms
    scale = slots ** (-0.5)
    readout = channels ** (-0.25)
    f32, bf16 = jnp.float32, jnp.bfloat16

    def pieces(chunk, own):
        parts = []
        for which, ref in enumerate(ghosts):
            for block in range(blocks[which]):
                if which == 0 and block == 0:
                    parts.append(own)
                else:
                    at = block * packet + chunk * atoms
                    parts.append(ref[at : at + atoms, :])
        return jnp.concatenate(parts, axis=0)

    picks, contrast = picks_in[...], contrast_in[...]

    row = 0
    for which, ref in enumerate(ghosts):
        for block in range(blocks[which]):
            at = block * packet + chunks * atoms
            if row:
                place_rows[:, row : row + atoms] = ref[at : at + atoms, 0:atoms]
            else:
                place_rows[0:3, 0:atoms] = places[...]
                place_rows[3:, 0:atoms] = jnp.zeros((atoms - 3, atoms), f32)
            row += atoms
    apart = joined(dot(thirds(place_rows[...]), contrast, (1, 0)), 8) + displace[...]
    distance = jnp.sqrt(jnp.sum(apart * apart, axis=0, keepdims=True) + SOFTENING)
    direction = apart / distance
    centres = FIRST_CENTRE + SPACING * lax.broadcasted_iota(jnp.int32, (first.shape[0], edges), 0).astype(f32)
    off = distance - centres
    gauss = jnp.exp(-SHARPNESS * off * off)
    basis = jnp.concatenate([gauss, gauss * off * (-2.0 * SHARPNESS)], axis=1)
    hidden = dot(first[...], basis.astype(bf16), (0, 0))
    for layer in (second[...], None):
        value, slope = hidden[:, 0:edges], hidden[:, edges:]
        sig = sigmoid(value)
        value, slope = value * sig, slope * sig * (1.0 + value * (1.0 - sig))
        if layer is None:
            value, slope = value * usable[...], slope * usable[...]
        hidden = jnp.concatenate([value, slope], axis=1).astype(bf16)
        if layer is not None:
            hidden = dot(layer, hidden, (0, 0))
    weights[0:edges, :] = dot(hidden[:, 0:edges], third[...], (0, 0))
    spread = (
        lax.broadcasted_iota(jnp.int32, (8, 3 * LANES), 1) // LANES
        == lax.broadcasted_iota(jnp.int32, (8, 3 * LANES), 0)
    ).astype(f32).astype(bf16)
    steer[...] = dot(direction.astype(bf16), spread, (0, 0))

    table = []
    for part in range(4):
        for h in range(halves):
            lanes = slice(h * LANES, (h + 1) * LANES)
            own = scalars[:, lanes] if part == 0 else vectors[part - 1, :, lanes]
            table.append(pieces(part * halves + h, own).astype(bf16))
    far[...] = dot(picks, jnp.concatenate(table, axis=1), (0, 0))

    tile = 2 * atoms
    steps = edges // tile
    third_part = jnp.asarray(1.0 / 3.0, bf16)

    def edge_inputs(step, h, kind):
        at = slice(step * tile, (step + 1) * tile)
        s = far[at, h * LANES : (h + 1) * LANES].astype(kind)
        v = [far[at, ((1 + a) * halves + h) * LANES : ((1 + a) * halves + h + 1) * LANES].astype(kind) for a in range(3)]
        u = [steer[at, a * LANES : (a + 1) * LANES].astype(kind) for a in range(3)]
        w = [weights[at, n * channels + h * LANES : n * channels + (h + 1) * LANES].astype(kind) for n in range(6)]
        return at, s, v, u, w

    def slopes(step, h, kind):
        at = slice(edges + step * tile, edges + (step + 1) * tile)
        return [weights[at, n * channels + h * LANES : n * channels + (h + 1) * LANES].astype(kind) for n in range(6)]

    def cross(a, b):
        return [a[1] * b[2] - a[2] * b[1], a[2] * b[0] - a[0] * b[2], a[0] * b[1] - a[1] * b[0]]

    def inner(a, b):
        return a[0] * b[0] + a[1] * b[1] + a[2] * b[2]

    def stacked(values, first, last):
        return jnp.concatenate([jnp.concatenate(values[n], axis=0) for n in range(first, last)], axis=1)

    messages = [[] for _ in range(chunks)]
    for step in range(steps):
        for h in range(halves):
            at, s, v, u, w = edge_inputs(step, h, f32)
            q = inner(u, v)
            along = w[2] * s + w[5] * q
            keep = w[3] - w[5] * third_part.astype(w[5].dtype)
            turned = cross([w[4] * x for x in v], u)
            new = [w[0] * s + w[1] * q] + [along * u[a] + keep * v[a] + turned[a] for a in range(3)]
            for part, value in enumerate(new):
                messages[part * halves + h].append(value.astype(bf16))
    weights[edges:, :] = dot(hidden[:, edges:], third[...], (0, 0))
    centre = lax.broadcasted_iota(jnp.int32, (atoms, edges), 1) % atoms
    mine = (centre == lax.broadcasted_iota(jnp.int32, (atoms, edges), 0)).astype(f32).astype(bf16)
    summed = dot(mine, stacked(messages, 0, chunks), (1, 0))

    cotangents = []
    terms = []
    for h in range(halves):
        lanes = slice(h * LANES, (h + 1) * LANES)
        sums = [summed[:, (p * halves + h) * LANES : (p * halves + h + 1) * LANES] for p in range(4)]
        s_out = scalars[:, lanes] + scale * sums[0]
        v_out = [vectors[a, :, lanes] + scale * sums[1 + a] for a in range(3)]
        c = coeff[:, lanes]
        g = gains[:, lanes]
        sig = sigmoid(s_out)
        terms.append(c * s_out * sig + g * inner(v_out, v_out))
        cot_s = readout * c * sig * (1.0 + s_out * (1.0 - sig))
        cot_v = [(2.0 * readout) * g * v_out[a] for a in range(3)]
        cotangents.append([cot_s] + cot_v)
    total = sum(terms[1:], terms[0])
    energies[...] = readout * dot(jnp.ones((8, LANES), f32), total, (1, 1), HIGHEST)[0:1, :]

    dfar, dsteer = [[[] for _ in range(n * halves)] for n in (4, 5)]
    pulled = [[(scale * jnp.concatenate([x, x], axis=0)).astype(bf16) for x in c] for c in cotangents]
    for step in range(steps):
        for h in range(halves):
            at, s, v, u, w = edge_inputs(step, h, bf16)
            cs, *cv = pulled[h]
            q = inner(u, v)
            along = w[2] * s + w[5] * q
            keep = w[3] - w[5] * third_part.astype(w[5].dtype)
            d = inner(cv, u)
            turn = cross(u, cv)
            spin = cross(cv, v)
            dq = cs * w[1] + w[5] * d
            ds = cs * w[0] + w[2] * d
            dv = [dq * u[a] + keep * cv[a] + w[4] * turn[a] for a in range(3)]
            du = [dq * v[a] + along * cv[a] + w[4] * spin[a] for a in range(3)]
            g = slopes(step, h, bf16)
            stretch = [
                s * (cs * g[0] + d * g[2]) + q * (cs * g[1] + d * g[5]),
                inner(cv, v) * (g[3] - g[5] * third_part.astype(g[5].dtype)) + inner(u, spin) * g[4],
            ]
            for part, value in enumerate([ds] + dv):
                dfar[part * halves + h].append(value.astype(bf16))
            for a, value in enumerate(du + stretch):
                dsteer[a * halves + h].append(value.astype(bf16))

    def put(chunk, value):
        for members, ref in zip(sinks, grads):
            for n, block in enumerate(members):
                piece = value[block * atoms : (block + 1) * atoms, :]
                at = (n * chunks + chunk) * atoms
                if block == 0:
                    piece = piece + cotangents[chunk % halves][chunk // halves]
                    own_out[chunk * atoms : (chunk + 1) * atoms, :] = piece
                    piece = jnp.zeros_like(piece)
                ref[at : at + atoms, :] = piece

    for chunk in range(chunks):
        put(chunk, dot(picks, stacked(dfar, chunk, chunk + 1), (1, 0)))

    gather = (
        jnp.minimum(lax.broadcasted_iota(jnp.int32, (8, 5 * channels), 1) // channels, 3)
        == lax.broadcasted_iota(jnp.int32, (8, 5 * channels), 0)
    ).astype(f32).astype(bf16)
    ddirection = dot(gather, stacked(dsteer, 0, 5 * halves), (1, 1))
    ddistance = ddirection[3:4, :]
    radial = jnp.sum(ddirection * direction, axis=0, keepdims=True)
    inv = 1.0 / distance
    component = lax.broadcasted_iota(jnp.int32, (8, edges), 0) < 3
    dapart = jnp.where(component, ddirection * inv, 0.0) + (ddistance - radial * inv) * direction
    dspots = joined(dot(thirds(dapart), contrast, (1, 1)), 8)

    for members, ref in zip(sinks, grads):
        at = len(members) * chunks * atoms
        ref[at:, :] = jnp.zeros((atoms, LANES), f32)
        for n, block in enumerate(members):
            piece = dspots[:, block * atoms : (block + 1) * atoms]
            if block == 0:
                own_out[chunks * atoms :, :] = jnp.zeros((atoms, LANES), f32)
                own_out[chunks * atoms :, 0:atoms] = piece
            else:
                ref[at:, n * atoms : (n + 1) * atoms] = piece


def finish_kernel(energies_in, own, lands, *rest):
    parts = rest[:-8]
    energies, forces, grad_scalars, grad_vectors, moved, scalar_rows, vector_rows, sems = rest[-8:]
    atoms, channels = scalar_rows.shape
    halves = channels // LANES
    chunks = 4 * halves
    copies = [
        pltpu.make_async_copy(a, b, sems.at[n])
        for n, (a, b) in enumerate([
            (energies_in, energies), (moved, forces), (scalar_rows, grad_scalars), (vector_rows, grad_vectors),
        ])
    ]
    copies[0].start()
    values = [ref[0 : chunks * atoms, :] for ref in parts]
    value = sum(values[1:], values[0])
    spots = [ref[ref.shape[0] - atoms :, n * atoms : (n + 1) * atoms] for n, ref in enumerate(parts)]
    spots = sum(spots[1:], spots[0])
    ghost = [value[c * atoms : (c + 1) * atoms, :] for c in range(chunks)]
    land = lands[...].astype(jnp.bfloat16)
    sums = dot(land, thirds(jnp.concatenate(ghost, axis=1)), (1, 0))
    for part in (1, 2, 3, 0):
        for h in range(halves):
            chunk = part * halves + h
            total = own[chunk * atoms : (chunk + 1) * atoms, :] + sums[:, chunk * LANES : (chunk + 1) * LANES]
            lanes = slice(h * LANES, (h + 1) * LANES)
            if part:
                vector_rows[part - 1, :, lanes] = total
            else:
                scalar_rows[:, lanes] = total
        if part == 3:
            copies[3].start()
    copies[2].start()
    spots = joined(dot(thirds(spots), land[:, 0:atoms], (1, 1)), atoms)
    moved[...] = -(own[chunks * atoms :, 0:atoms] + spots)[0:3, :]
    copies[1].start()
    for copy in copies:
        copy.wait()


VMEM = pl.BlockSpec(memory_space=pltpu.VMEM)
SMEM = pl.BlockSpec(memory_space=pltpu.SMEM)


def shards(
    places, scalars, vectors, species, bound_rows, bound_count, neighbour_ids, neighbour_count,
    radial_first, radial_second, radial_third, energy_table, vector_gains,
):
    f32 = jnp.float32
    atoms, channels = scalars.shape
    places, vectors = places.T, vectors.transpose(1, 0, 2)
    boundary = bound_rows.shape[0]
    assert boundary == atoms == 8
    slots = neighbour_ids.shape[0]
    edges = slots * atoms
    halves = channels // LANES
    chunks = 4 * halves
    packet_rows = (chunks + 1) * boundary

    packet = pl.pallas_call(
        pack_kernel,
        out_shape=jax.ShapeDtypeStruct((packet_rows, LANES), f32),
        in_specs=[SMEM] + [pl.BlockSpec(memory_space=pltpu.HBM)] * 4,
        out_specs=VMEM,
        scratch_shapes=[
            pltpu.SMEM(bound_rows.shape, jnp.int32),
            pltpu.VMEM(places.shape, f32),
            pltpu.VMEM(scalars.shape, f32),
            pltpu.VMEM(vectors.shape, f32),
            pltpu.SemaphoreType.DMA((4,)),
        ],
        compiler_params=pltpu.CompilerParams(vmem_limit_bytes=2 << 20),
        name="pack",
    )(bound_count, *[pltpu.with_memory_space_constraint(x, pltpu.HBM) for x in (bound_rows, places, scalars, vectors)])

    perms = {axis: sides(lax.axis_size(axis)) for axis in AXES}
    wide = {axis: 1 + len(perms[axis]) for axis in AXES}
    per_plane = wide["gx"] * wide["gy"]
    rows = per_plane * wide["gz"] * atoms
    beside_x = [lax.ppermute(packet, "gx", pairs) for pairs in perms["gx"]]
    beside_y = [lax.ppermute(packet, "gy", pairs) for pairs in perms["gy"]]
    across = jnp.concatenate(beside_x, axis=0)
    across, ids, counts = lax.optimization_barrier((across, neighbour_ids.T, neighbour_count.reshape(1, atoms)))
    plain = [
        places, scalars, vectors, radial_first, radial_second, radial_third, vector_gains.reshape(1, channels),
    ]
    parities = jnp.stack([lax.axis_index(a) % 2 if lax.axis_size(a) % 2 == 0 else 0 for a in AXES])
    prepared = pl.pallas_call(
        functools.partial(prep_kernel, tuple(wide[a] for a in AXES)),
        out_shape=[
            jax.ShapeDtypeStruct((rows, edges), jnp.bfloat16),
            jax.ShapeDtypeStruct((rows, edges), jnp.bfloat16),
            jax.ShapeDtypeStruct((8, edges), f32),
            jax.ShapeDtypeStruct((1, edges), f32),
            jax.ShapeDtypeStruct((atoms, channels), f32),
            jax.ShapeDtypeStruct((atoms, 3 * atoms), f32),
        ]
        + [jax.ShapeDtypeStruct(x.shape, x.dtype) for x in plain],
        in_specs=[SMEM] + [VMEM] * (6 + len(plain)),
        out_specs=[VMEM] * (6 + len(plain)),
        compiler_params=pltpu.CompilerParams(vmem_limit_bytes=2 << 20),
        name="prep",
    )(
        parities, ids, counts, species.reshape(1, atoms), energy_table,
        bound_rows.reshape(1, boundary), bound_count.reshape(1, 1), *plain,
    )
    prepared, plain = prepared[:6], prepared[6:]
    *prepared, lands = prepared
    corners = [lax.ppermute(across, "gy", pairs) for pairs in perms["gy"]]
    cross = jnp.concatenate([packet, across] + beside_y, axis=0)
    tables = [packet, across] + beside_y + corners
    for pairs in perms["gz"]:
        tables.append(lax.ppermute(cross, "gz", pairs))
        tables += [lax.ppermute(c, "gz", pairs) for c in corners]
    blocks = tuple(t.shape[0] // packet_rows for t in tables)
    nx, ny = wide["gx"], wide["gy"]
    sinks = []
    for z in range(wide["gz"]):
        first = z * per_plane
        sinks.append(tuple(range(first, first + nx)))
        for y in range(1, ny):
            corner = first + nx + ny - 1 + (y - 1) * (nx - 1)
            sinks.append((first + nx + y - 1, *range(corner, corner + nx - 1)))

    geometry = (atoms, slots, channels, blocks, tuple(sinks))
    out = pl.pallas_call(
        functools.partial(core_kernel, geometry),
        out_shape=[
            jax.ShapeDtypeStruct((1, atoms), f32),
            jax.ShapeDtypeStruct(((chunks + 1) * atoms, LANES), f32),
        ]
        + [jax.ShapeDtypeStruct(((len(n) * chunks + 1) * boundary, LANES), f32) for n in sinks],
        in_specs=[VMEM] * (12 + len(tables)),
        out_specs=[VMEM] * (2 + len(sinks)),
        scratch_shapes=[
            pltpu.VMEM((2 * edges, 6 * channels), f32),
            pltpu.VMEM((edges, chunks * LANES), f32),
            pltpu.VMEM((edges, 3 * LANES), f32),
            pltpu.VMEM((atoms, rows), f32),
        ],
        compiler_params=pltpu.CompilerParams(vmem_limit_bytes=16 << 20),
        name="edges",
    )(
        *prepared, *plain, *tables,
    )
    energies, own, *grads = out

    lines = grads[:ny]
    for n, pairs in enumerate(perms["gz"]):
        back = [lax.ppermute(grads[(n + 1) * ny + y], "gz", inverse(pairs)) for y in range(ny)]
        lines = [a + b for a, b in zip(lines, back)]
    line = lines[0]
    for n, pairs in enumerate(perms["gy"]):
        line = line + lax.ppermute(lines[n + 1], "gy", inverse(pairs))
    parts, span = [line], chunks * boundary
    for n, pairs in enumerate(perms["gx"]):
        value = jnp.concatenate([line[(n + 1) * span : (n + 2) * span], line[-boundary:]], axis=0)
        parts.append(lax.ppermute(value, "gx", inverse(pairs)))

    energies, forces, grad_scalars, grad_vectors = pl.pallas_call(
        finish_kernel,
        out_shape=[
            jax.ShapeDtypeStruct((1, atoms), f32),
            jax.ShapeDtypeStruct((3, atoms), f32),
            jax.ShapeDtypeStruct((atoms, channels), f32),
            jax.ShapeDtypeStruct((3, atoms, channels), f32),
        ],
        in_specs=[VMEM] * (3 + len(parts)),
        out_specs=[pl.BlockSpec(memory_space=pltpu.HBM)] * 4,
        scratch_shapes=[
            pltpu.VMEM((3, atoms), f32),
            pltpu.VMEM((atoms, channels), f32),
            pltpu.VMEM((3, atoms, channels), f32),
            pltpu.SemaphoreType.DMA((4,)),
        ],
        compiler_params=pltpu.CompilerParams(vmem_limit_bytes=2 << 20),
        name="finish",
    )(energies, own, lands, *parts)
    return energies.reshape(atoms), forces.T, grad_scalars, grad_vectors.transpose(1, 0, 2)


def solution(mesh):
    every = AXES
    in_specs = (
        P(every, None), P(every, None), P(every, None, None), P(every), P(every), P(every),
        P(None, every), P(every), P(), P(), P(), P(), P(),
    )
    out_specs = (P(every), P(every, None), P(every, None), P(every, None, None))

    return jax.shard_map(shards, mesh=mesh, in_specs=in_specs, out_specs=out_specs, check_vma=False)
```

```python
import functools

import jax
import jax.numpy as jnp
from jax import lax
from jax.experimental import pallas as pl
from jax.experimental.pallas import tpu as pltpu
from jax.sharding import PartitionSpec as P


SOFTENING = 0.25
SHARPNESS = 2.0
FIRST_CENTRE = 0.5
SPACING = 0.4
EDGE = 1.0
LANES = 128
HIGHEST = lax.Precision.HIGHEST
AXES = ("gx", "gy", "gz")


def dot(a, b, dims, precision=None):
    return lax.dot_general(
        a, b, ((dims[:1], dims[1:]), ((), ())), precision=precision,
        preferred_element_type=jnp.float32,
    )


def thirds(x, axis=0):
    high = x.astype(jnp.bfloat16).astype(jnp.float32)
    rest = x - high
    middle = rest.astype(jnp.bfloat16).astype(jnp.float32)
    return jnp.concatenate([high, middle, rest - middle], axis=axis).astype(jnp.bfloat16)


def joined(x, rows):
    return x[0:rows, :] + (x[rows : 2 * rows, :] + x[2 * rows :, :])


def sides(size):
    if size == 1:
        return []
    if size == 2:
        return [[(0, 1), (1, 0)]]
    if size % 2:
        return [[((i + 1) % size, i) for i in range(size)], [(i, (i + 1) % size) for i in range(size)]]
    pairs = [[(i, (i + 1) % size) for i in range(first, size, 2)] for first in (0, 1)]
    return [half + [(b, a) for a, b in half] for half in pairs]


def inverse(pairs):
    return [(b, a) for a, b in pairs]


def pack_kernel(
    bound_count, bound_rows_in, places_in, scalars_in, vectors_in, out,
    bound_rows, places, scalars, vectors, sems,
):
    pairs = [(bound_rows_in, bound_rows), (places_in, places), (scalars_in, scalars), (vectors_in, vectors)]
    copies = [pltpu.make_async_copy(a, b, sems.at[n]) for n, (a, b) in enumerate(pairs)]
    for copy in copies:
        copy.start()
    boundary = bound_rows.shape[0]
    halves = scalars.shape[1] // LANES
    source = lax.broadcasted_iota(jnp.int32, (places.shape[1], LANES), 0)
    lane = lax.broadcasted_iota(jnp.int32, (places.shape[1], LANES), 1)
    moved = jnp.zeros(source.shape, jnp.float32)
    copies[0].wait()
    atoms = [bound_rows[slot] for slot in range(boundary)]
    alive = [jnp.where(slot < bound_count[0], 1.0, 0.0).astype(jnp.float32) for slot in range(boundary)]
    for slot in range(boundary):
        moved = jnp.where((lane == slot) & (source == atoms[slot]), alive[slot], moved)
    copies[1].wait()
    spots = joined(dot(thirds(jnp.concatenate([places[...], jnp.zeros((5, source.shape[0]), jnp.float32)], axis=0)),
                       moved.astype(jnp.bfloat16), (1, 0)), 8)
    copies[2].wait()
    copies[3].wait()
    for slot in range(boundary):
        rows = [scalars[pl.ds(atoms[slot], 1), :]] + [vectors[a, pl.ds(atoms[slot], 1), :] for a in range(3)]
        for part, row in enumerate(rows):
            row = row * alive[slot]
            for h in range(halves):
                at = (part * halves + h) * boundary + slot
                out[at : at + 1, :] = row[:, h * LANES : (h + 1) * LANES]
    out[4 * halves * boundary :, :] = spots


def prep_kernel(
    wide, parities, ids, counts, species, energy_table, bound_rows, bound_count, *rest
):
    atoms, slots = ids.shape
    edges = atoms * slots
    f32 = jnp.float32
    count = (len(rest) - 6) // 2
    passed, (picks, contrast, displace, usable, coeff, lands), copied = rest[:count], rest[count:-count], rest[-count:]
    for a, b in zip(passed, copied):
        b[...] = a[...]
    lane = lax.broadcasted_iota(jnp.int32, (atoms, edges), 1)
    mine = lane % atoms == lax.broadcasted_iota(jnp.int32, (atoms, edges), 0)
    slot_lane = lax.broadcasted_iota(jnp.int32, (slots, edges), 1) // atoms
    belongs = (slot_lane == lax.broadcasted_iota(jnp.int32, (slots, edges), 0)).astype(f32)
    spread = dot(ids[...].astype(f32), belongs, (1, 0), HIGHEST)
    where = jnp.sum(jnp.where(mine, spread, 0.0), axis=0, keepdims=True).astype(jnp.int32)
    live = dot(jnp.broadcast_to(counts[...], (8, atoms)).astype(f32), mine.astype(f32), (1, 0), HIGHEST)[0:1, :]
    usable[...] = (slot_lane[0:1, :].astype(f32) < live).astype(f32)
    owned = where < atoms
    ghost = jnp.maximum(where - atoms, 0)
    block = ghost // atoms
    offsets = [block // 9 - 1, (block // 3) % 3 - 1, block % 3 - 1]
    at = []
    for axis, offset in enumerate(offsets):
        if wide[axis] == 1:
            at.append(jnp.zeros_like(offset))
        elif wide[axis] == 2:
            at.append(jnp.abs(offset))
        else:
            at.append(jnp.where(offset == 0, 0, jnp.where(offset == 1 - 2 * parities[axis], 1, 2)))
    inside = jnp.where(
        at[1] == 0, at[0],
        jnp.where(at[0] == 0, wide[0] - 1 + at[1], wide[0] + wide[1] - 1 + (at[1] - 1) * (wide[0] - 1) + at[0] - 1),
    )
    stored = at[2] * (wide[0] * wide[1]) + inside
    row_of = jnp.where(owned, where, stored * atoms + ghost % atoms)
    row_index = lax.broadcasted_iota(jnp.int32, contrast.shape, 0)
    centre = lax.broadcasted_iota(jnp.int32, contrast.shape, 1) % atoms
    chosen = (row_index == row_of).astype(f32)
    picks[...] = chosen.astype(jnp.bfloat16)
    contrast[...] = (chosen - (row_index == centre).astype(f32)).astype(jnp.bfloat16)
    kinds = (lax.broadcasted_iota(jnp.int32, (energy_table.shape[0], atoms), 0) == species[...]).astype(f32)
    coeff[...] = dot(kinds, energy_table[...], (0, 0), HIGHEST)
    slot = lax.broadcasted_iota(jnp.int32, (atoms, atoms), 1)
    target = lax.broadcasted_iota(jnp.int32, (atoms, atoms), 0)
    land = ((target == bound_rows[...]) & (slot < bound_count[...])).astype(f32)
    lands[...] = jnp.concatenate([land, land, land], axis=1)
    shift = [jnp.where(owned, 0, offset).astype(f32) * EDGE for offset in offsets]
    displace[...] = jnp.concatenate(shift + [jnp.zeros((5, edges), f32)], axis=0)


def sigmoid(x):
    return 1.0 / (1.0 + jnp.exp(-x))


def core_kernel(
    geometry,
    picks_in, contrast_in, displace, usable, coeff, places, scalars, vectors, first, second, third,
    gains, *rest,
):
    atoms, slots, channels, blocks, sinks = geometry
    tables = len(blocks)
    ghosts = rest[:tables]
    energies, own_out = rest[tables : tables + 2]
    grads = rest[tables + 2 : tables + 2 + len(sinks)]
    weights, far, steer, place_rows = rest[tables + 2 + len(sinks) :]
    halves = channels // LANES
    chunks = 4 * halves
    edges = atoms * slots
    packet = (chunks + 1) * atoms
    scale = slots ** (-0.5)
    readout = channels ** (-0.25)
    f32, bf16 = jnp.float32, jnp.bfloat16

    def pieces(chunk, own):
        parts = []
        for which, ref in enumerate(ghosts):
            for block in range(blocks[which]):
                if which == 0 and block == 0:
                    parts.append(own)
                else:
                    at = block * packet + chunk * atoms
                    parts.append(ref[at : at + atoms, :])
        return jnp.concatenate(parts, axis=0)

    picks, contrast = picks_in[...], contrast_in[...]

    row = 0
    for which, ref in enumerate(ghosts):
        for block in range(blocks[which]):
            at = block * packet + chunks * atoms
            if row:
                place_rows[:, row : row + atoms] = ref[at : at + atoms, 0:atoms]
            else:
                place_rows[0:3, 0:atoms] = places[...]
                place_rows[3:, 0:atoms] = jnp.zeros((atoms - 3, atoms), f32)
            row += atoms
    apart = joined(dot(thirds(place_rows[...]), contrast, (1, 0)), 8) + displace[...]
    distance = jnp.sqrt(jnp.sum(apart * apart, axis=0, keepdims=True) + SOFTENING)
    direction = apart / distance
    centres = FIRST_CENTRE + SPACING * lax.broadcasted_iota(jnp.int32, (first.shape[0], edges), 0).astype(f32)
    off = distance - centres
    gauss = jnp.exp(-SHARPNESS * off * off)
    basis = jnp.concatenate([gauss, gauss * off * (-2.0 * SHARPNESS)], axis=1)
    hidden = dot(first[...], basis.astype(bf16), (0, 0))
    for layer in (second[...], None):
        value, slope = hidden[:, 0:edges], hidden[:, edges:]
        sig = sigmoid(value)
        value, slope = value * sig, slope * sig * (1.0 + value * (1.0 - sig))
        if layer is None:
            value, slope = value * usable[...], slope * usable[...]
        hidden = jnp.concatenate([value, slope], axis=1).astype(bf16)
        if layer is not None:
            hidden = dot(layer, hidden, (0, 0))
    weights[0:edges, :] = dot(hidden[:, 0:edges], third[...], (0, 0))
    spread = (
        lax.broadcasted_iota(jnp.int32, (8, 3 * LANES), 1) // LANES
        == lax.broadcasted_iota(jnp.int32, (8, 3 * LANES), 0)
    ).astype(f32).astype(bf16)
    steer[...] = dot(direction.astype(bf16), spread, (0, 0))

    table = []
    for part in range(4):
        for h in range(halves):
            lanes = slice(h * LANES, (h + 1) * LANES)
            own = scalars[:, lanes] if part == 0 else vectors[part - 1, :, lanes]
            table.append(pieces(part * halves + h, own).astype(bf16))
    far[...] = dot(picks, jnp.concatenate(table, axis=1), (0, 0))

    tile = 2 * atoms
    steps = edges // tile
    third_part = jnp.asarray(1.0 / 3.0, bf16)

    def edge_inputs(step, h):
        at = slice(step * tile, (step + 1) * tile)
        s = far[at, h * LANES : (h + 1) * LANES].astype(bf16)
        v = [far[at, ((1 + a) * halves + h) * LANES : ((1 + a) * halves + h + 1) * LANES].astype(bf16) for a in range(3)]
        u = [steer[at, a * LANES : (a + 1) * LANES].astype(bf16) for a in range(3)]
        w = [weights[at, n * channels + h * LANES : n * channels + (h + 1) * LANES].astype(bf16) for n in range(6)]
        return at, s, v, u, w

    def slopes(step, h):
        at = slice(edges + step * tile, edges + (step + 1) * tile)
        return [weights[at, n * channels + h * LANES : n * channels + (h + 1) * LANES].astype(bf16) for n in range(6)]

    def cross(a, b):
        return [a[1] * b[2] - a[2] * b[1], a[2] * b[0] - a[0] * b[2], a[0] * b[1] - a[1] * b[0]]

    def inner(a, b):
        return a[0] * b[0] + a[1] * b[1] + a[2] * b[2]

    def stacked(values, first, last):
        return jnp.concatenate([jnp.concatenate(values[n], axis=0) for n in range(first, last)], axis=1)

    messages = [[] for _ in range(chunks)]
    for step in range(steps):
        for h in range(halves):
            at, s, v, u, w = edge_inputs(step, h)
            q = inner(u, v)
            along = w[2] * s + w[5] * q
            keep = w[3] - w[5] * third_part
            turned = cross([w[4] * x for x in v], u)
            new = [w[0] * s + w[1] * q] + [along * u[a] + keep * v[a] + turned[a] for a in range(3)]
            for part, value in enumerate(new):
                messages[part * halves + h].append(value)
    weights[edges:, :] = dot(hidden[:, edges:], third[...], (0, 0))
    centre = lax.broadcasted_iota(jnp.int32, (atoms, edges), 1) % atoms
    mine = (centre == lax.broadcasted_iota(jnp.int32, (atoms, edges), 0)).astype(f32).astype(bf16)
    summed = dot(mine, stacked(messages, 0, chunks), (1, 0))

    cotangents = []
    terms = []
    for h in range(halves):
        lanes = slice(h * LANES, (h + 1) * LANES)
        sums = [summed[:, (p * halves + h) * LANES : (p * halves + h + 1) * LANES] for p in range(4)]
        s_out = scalars[:, lanes] + scale * sums[0]
        v_out = [vectors[a, :, lanes] + scale * sums[1 + a] for a in range(3)]
        c = coeff[:, lanes]
        g = gains[:, lanes]
        sig = sigmoid(s_out)
        terms.append(c * s_out * sig + g * inner(v_out, v_out))
        cot_s = readout * c * sig * (1.0 + s_out * (1.0 - sig))
        cot_v = [(2.0 * readout) * g * v_out[a] for a in range(3)]
        cotangents.append([cot_s] + cot_v)
    total = sum(terms[1:], terms[0])
    energies[...] = readout * dot(jnp.ones((8, LANES), f32), total, (1, 1), HIGHEST)[0:1, :]

    dfar, dsteer = [[[] for _ in range(n * halves)] for n in (4, 5)]
    pulled = [[(scale * jnp.concatenate([x, x], axis=0)).astype(bf16) for x in c] for c in cotangents]
    for step in range(steps):
        for h in range(halves):
            at, s, v, u, w = edge_inputs(step, h)
            cs, *cv = pulled[h]
            q = inner(u, v)
            along = w[2] * s + w[5] * q
            keep = w[3] - w[5] * third_part
            d = inner(cv, u)
            turn = cross(u, cv)
            spin = cross(cv, v)
            dq = cs * w[1] + w[5] * d
            ds = cs * w[0] + w[2] * d
            dv = [dq * u[a] + keep * cv[a] + w[4] * turn[a] for a in range(3)]
            du = [dq * v[a] + along * cv[a] + w[4] * spin[a] for a in range(3)]
            g = slopes(step, h)
            stretch = [
                s * (cs * g[0] + d * g[2]) + q * (cs * g[1] + d * g[5]),
                inner(cv, v) * (g[3] - g[5] * third_part) + inner(u, spin) * g[4],
            ]
            for part, value in enumerate([ds] + dv):
                dfar[part * halves + h].append(value)
            for a, value in enumerate(du + stretch):
                dsteer[a * halves + h].append(value)

    def put(chunk, value):
        for members, ref in zip(sinks, grads):
            for n, block in enumerate(members):
                piece = value[block * atoms : (block + 1) * atoms, :]
                at = (n * chunks + chunk) * atoms
                if block == 0:
                    piece = piece + cotangents[chunk % halves][chunk // halves]
                    own_out[chunk * atoms : (chunk + 1) * atoms, :] = piece
                    piece = jnp.zeros_like(piece)
                ref[at : at + atoms, :] = piece

    for chunk in range(chunks):
        put(chunk, dot(picks, stacked(dfar, chunk, chunk + 1), (1, 0)))

    gather = (
        jnp.minimum(lax.broadcasted_iota(jnp.int32, (8, 5 * channels), 1) // channels, 3)
        == lax.broadcasted_iota(jnp.int32, (8, 5 * channels), 0)
    ).astype(f32).astype(bf16)
    ddirection = dot(gather, stacked(dsteer, 0, 5 * halves), (1, 1))
    ddistance = ddirection[3:4, :]
    radial = jnp.sum(ddirection * direction, axis=0, keepdims=True)
    inv = 1.0 / distance
    component = lax.broadcasted_iota(jnp.int32, (8, edges), 0) < 3
    dapart = jnp.where(component, ddirection * inv, 0.0) + (ddistance - radial * inv) * direction
    dspots = joined(dot(thirds(dapart), contrast, (1, 1)), 8)

    for members, ref in zip(sinks, grads):
        at = len(members) * chunks * atoms
        ref[at:, :] = jnp.zeros((atoms, LANES), f32)
        for n, block in enumerate(members):
            piece = dspots[:, block * atoms : (block + 1) * atoms]
            if block == 0:
                own_out[chunks * atoms :, :] = jnp.zeros((atoms, LANES), f32)
                own_out[chunks * atoms :, 0:atoms] = piece
            else:
                ref[at:, n * atoms : (n + 1) * atoms] = piece


def finish_kernel(energies_in, own, lands, *rest):
    parts = rest[:-8]
    energies, forces, grad_scalars, grad_vectors, moved, scalar_rows, vector_rows, sems = rest[-8:]
    atoms, channels = scalar_rows.shape
    halves = channels // LANES
    chunks = 4 * halves
    copies = [
        pltpu.make_async_copy(a, b, sems.at[n])
        for n, (a, b) in enumerate([
            (energies_in, energies), (moved, forces), (scalar_rows, grad_scalars), (vector_rows, grad_vectors),
        ])
    ]
    copies[0].start()
    values = [ref[0 : chunks * atoms, :] for ref in parts]
    value = sum(values[1:], values[0])
    spots = [ref[ref.shape[0] - atoms :, n * atoms : (n + 1) * atoms] for n, ref in enumerate(parts)]
    spots = sum(spots[1:], spots[0])
    ghost = [value[c * atoms : (c + 1) * atoms, :] for c in range(chunks)]
    land = lands[...].astype(jnp.bfloat16)
    sums = dot(land, thirds(jnp.concatenate(ghost, axis=1)), (1, 0))
    for part in (1, 2, 3, 0):
        for h in range(halves):
            chunk = part * halves + h
            total = own[chunk * atoms : (chunk + 1) * atoms, :] + sums[:, chunk * LANES : (chunk + 1) * LANES]
            lanes = slice(h * LANES, (h + 1) * LANES)
            if part:
                vector_rows[part - 1, :, lanes] = total
            else:
                scalar_rows[:, lanes] = total
        if part == 3:
            copies[3].start()
    copies[2].start()
    spots = joined(dot(thirds(spots), land[:, 0:atoms], (1, 1)), atoms)
    moved[...] = -(own[chunks * atoms :, 0:atoms] + spots)[0:3, :]
    copies[1].start()
    for copy in copies:
        copy.wait()


VMEM = pl.BlockSpec(memory_space=pltpu.VMEM)
SMEM = pl.BlockSpec(memory_space=pltpu.SMEM)


def shards(
    places, scalars, vectors, species, bound_rows, bound_count, neighbour_ids, neighbour_count,
    radial_first, radial_second, radial_third, energy_table, vector_gains,
):
    f32 = jnp.float32
    atoms, channels = scalars.shape
    places, vectors = places.T, vectors.transpose(1, 0, 2)
    boundary = bound_rows.shape[0]
    assert boundary == atoms == 8
    slots = neighbour_ids.shape[0]
    edges = slots * atoms
    halves = channels // LANES
    chunks = 4 * halves
    packet_rows = (chunks + 1) * boundary

    packet = pl.pallas_call(
        pack_kernel,
        out_shape=jax.ShapeDtypeStruct((packet_rows, LANES), f32),
        in_specs=[SMEM] + [pl.BlockSpec(memory_space=pltpu.HBM)] * 4,
        out_specs=VMEM,
        scratch_shapes=[
            pltpu.SMEM(bound_rows.shape, jnp.int32),
            pltpu.VMEM(places.shape, f32),
            pltpu.VMEM(scalars.shape, f32),
            pltpu.VMEM(vectors.shape, f32),
            pltpu.SemaphoreType.DMA((4,)),
        ],
        compiler_params=pltpu.CompilerParams(vmem_limit_bytes=2 << 20),
        name="pack",
    )(bound_count, *[pltpu.with_memory_space_constraint(x, pltpu.HBM) for x in (bound_rows, places, scalars, vectors)])

    perms = {axis: sides(lax.axis_size(axis)) for axis in AXES}
    wide = {axis: 1 + len(perms[axis]) for axis in AXES}
    per_plane = wide["gx"] * wide["gy"]
    rows = per_plane * wide["gz"] * atoms
    beside_x = [lax.ppermute(packet, "gx", pairs) for pairs in perms["gx"]]
    beside_y = [lax.ppermute(packet, "gy", pairs) for pairs in perms["gy"]]
    across = jnp.concatenate(beside_x, axis=0)
    across, ids, counts = lax.optimization_barrier((across, neighbour_ids.T, neighbour_count.reshape(1, atoms)))
    plain = [
        places, scalars, vectors, radial_first, radial_second, radial_third, vector_gains.reshape(1, channels),
    ]
    parities = jnp.stack([lax.axis_index(a) % 2 if lax.axis_size(a) % 2 == 0 else 0 for a in AXES])
    prepared = pl.pallas_call(
        functools.partial(prep_kernel, tuple(wide[a] for a in AXES)),
        out_shape=[
            jax.ShapeDtypeStruct((rows, edges), jnp.bfloat16),
            jax.ShapeDtypeStruct((rows, edges), jnp.bfloat16),
            jax.ShapeDtypeStruct((8, edges), f32),
            jax.ShapeDtypeStruct((1, edges), f32),
            jax.ShapeDtypeStruct((atoms, channels), f32),
            jax.ShapeDtypeStruct((atoms, 3 * atoms), f32),
        ]
        + [jax.ShapeDtypeStruct(x.shape, x.dtype) for x in plain],
        in_specs=[SMEM] + [VMEM] * (6 + len(plain)),
        out_specs=[VMEM] * (6 + len(plain)),
        compiler_params=pltpu.CompilerParams(vmem_limit_bytes=2 << 20),
        name="prep",
    )(
        parities, ids, counts, species.reshape(1, atoms), energy_table,
        bound_rows.reshape(1, boundary), bound_count.reshape(1, 1), *plain,
    )
    prepared, plain = prepared[:6], prepared[6:]
    *prepared, lands = prepared
    corners = [lax.ppermute(across, "gy", pairs) for pairs in perms["gy"]]
    cross = jnp.concatenate([packet, across] + beside_y, axis=0)
    tables = [packet, across] + beside_y + corners
    for pairs in perms["gz"]:
        tables.append(lax.ppermute(cross, "gz", pairs))
        tables += [lax.ppermute(c, "gz", pairs) for c in corners]
    blocks = tuple(t.shape[0] // packet_rows for t in tables)
    nx, ny = wide["gx"], wide["gy"]
    sinks = []
    for z in range(wide["gz"]):
        first = z * per_plane
        sinks.append(tuple(range(first, first + nx)))
        for y in range(1, ny):
            corner = first + nx + ny - 1 + (y - 1) * (nx - 1)
            sinks.append((first + nx + y - 1, *range(corner, corner + nx - 1)))

    geometry = (atoms, slots, channels, blocks, tuple(sinks))
    out = pl.pallas_call(
        functools.partial(core_kernel, geometry),
        out_shape=[
            jax.ShapeDtypeStruct((1, atoms), f32),
            jax.ShapeDtypeStruct(((chunks + 1) * atoms, LANES), f32),
        ]
        + [jax.ShapeDtypeStruct(((len(n) * chunks + 1) * boundary, LANES), f32) for n in sinks],
        in_specs=[VMEM] * (12 + len(tables)),
        out_specs=[VMEM] * (2 + len(sinks)),
        scratch_shapes=[
            pltpu.VMEM((2 * edges, 6 * channels), f32),
            pltpu.VMEM((edges, chunks * LANES), f32),
            pltpu.VMEM((edges, 3 * LANES), f32),
            pltpu.VMEM((atoms, rows), f32),
        ],
        compiler_params=pltpu.CompilerParams(vmem_limit_bytes=16 << 20),
        name="edges",
    )(
        *prepared, *plain, *tables,
    )
    energies, own, *grads = out

    lines = grads[:ny]
    for n, pairs in enumerate(perms["gz"]):
        back = [lax.ppermute(grads[(n + 1) * ny + y], "gz", inverse(pairs)) for y in range(ny)]
        lines = [a + b for a, b in zip(lines, back)]
    line = lines[0]
    for n, pairs in enumerate(perms["gy"]):
        line = line + lax.ppermute(lines[n + 1], "gy", inverse(pairs))
    parts, span = [line], chunks * boundary
    for n, pairs in enumerate(perms["gx"]):
        value = jnp.concatenate([line[(n + 1) * span : (n + 2) * span], line[-boundary:]], axis=0)
        parts.append(lax.ppermute(value, "gx", inverse(pairs)))

    energies, forces, grad_scalars, grad_vectors = pl.pallas_call(
        finish_kernel,
        out_shape=[
            jax.ShapeDtypeStruct((1, atoms), f32),
            jax.ShapeDtypeStruct((3, atoms), f32),
            jax.ShapeDtypeStruct((atoms, channels), f32),
            jax.ShapeDtypeStruct((3, atoms, channels), f32),
        ],
        in_specs=[VMEM] * (3 + len(parts)),
        out_specs=[pl.BlockSpec(memory_space=pltpu.HBM)] * 4,
        scratch_shapes=[
            pltpu.VMEM((3, atoms), f32),
            pltpu.VMEM((atoms, channels), f32),
            pltpu.VMEM((3, atoms, channels), f32),
            pltpu.SemaphoreType.DMA((4,)),
        ],
        compiler_params=pltpu.CompilerParams(vmem_limit_bytes=2 << 20),
        name="finish",
    )(energies, own, lands, *parts)
    return energies.reshape(atoms), forces.T, grad_scalars, grad_vectors.transpose(1, 0, 2)


def solution(mesh):
    every = AXES
    in_specs = (
        P(every, None), P(every, None), P(every, None, None), P(every), P(every), P(every),
        P(None, every), P(every), P(), P(), P(), P(), P(),
    )
    out_specs = (P(every), P(every, None), P(every, None), P(every, None, None))

    return jax.shard_map(shards, mesh=mesh, in_specs=in_specs, out_specs=out_specs, check_vma=False)
```
